512 devices in a mesh: blk: 8 (over y_lo, core), team: 64 (over y_hi, x, z).
Axes of the slice: x: 4, y: 8 (y_hi: 2, y_lo: 4; y = y_hi * 4 + y_lo), z: 8, core: 2. Of those that a mesh axis runs over, the one named last changes fastest.
Arguments:
- features: bfloat16 [65536, 256], P(('blk', 'team')), may hold values from -6 to 6
- weight: bfloat16 [256, 256], replicated, may hold values from -0.375 to 0.375
- bias: float32 [256], replicated, may hold values from -3 to 3
- cotangent: bfloat16 [65536, 256], P(('blk', 'team')), may hold values from -6 to 6
- adj_cols: int32 [64, 8, 8, 12], P('team', None, 'blk'), may hold values from 0 to 63, as said below
- adj_vals: bfloat16 [64, 8, 8, 12, 128, 128], P('team', None, 'blk'), as said below
Outputs:
- hidden: bfloat16 [65536, 256], P(('blk', 'team'))
- grad_input: bfloat16 [65536, 256], P(('blk', 'team'))
- grad_weight: float32 [256, 256], replicated
- grad_bias: float32 [256], replicated
The draws below stay inside these ranges and needn't reach their ends.
Inputs may be any that keep to these rules, and one draw needn't show every extreme that they name: `adj_cols`: for every node panel and column group the 12 entries are distinct. Block (i, j) of A is listed exactly when block (j, i) is, every column panel is listed by exactly 12 row panels of each column group, and A is symmetric. `adj_vals`: the block listed for panels (i, j) is the transpose of the block listed for (j, i), so A is symmetric.
All inputs are finite; a program needn't handle non-finite values.
Results may differ from the reference program's by a relative error of at most 0.0075.
Values may be sent and summed in bfloat16 or wider, within the bound.
No kernel may reach another device: no remote copies, remote signals or barrier semaphores. Data moves between devices by JAX's collectives and lax.ppermute only.
A program may use at most 64 MiB of HBM per device.

```python
import jax
import jax.numpy as jnp
from jax import lax

BLOCK = 128
WIDTH = 256
NNZ = 12
GROUPS = 8
MEMBERS = 64
NODES = 65536


def pattern_parts(key):
    perm_keys = jax.random.split(jax.random.fold_in(key, 101), GROUPS)
    perms = jax.vmap(lambda one: jax.random.permutation(one, MEMBERS))(perm_keys).astype(jnp.int32)
    inverse = jnp.argsort(perms, axis=1).astype(jnp.int32)
    row_groups = jnp.arange(GROUPS, dtype=jnp.int32)[:, None]
    col_groups = jnp.arange(GROUPS, dtype=jnp.int32)[None, :]
    pair_ids = (jnp.minimum(row_groups, col_groups) * GROUPS + jnp.maximum(row_groups, col_groups)).reshape(-1)
    offset_key = jax.random.fold_in(key, 102)
    offsets = jax.vmap(lambda pair: jax.random.permutation(jax.random.fold_in(offset_key, pair), MEMBERS)[:NNZ])(pair_ids)
    offsets = offsets.reshape(GROUPS, GROUPS, NNZ).astype(jnp.int32)
    shifted = (offsets[None, :, :, :] - perms.T[:, :, None, None]) % MEMBERS
    group_ids = jnp.arange(GROUPS, dtype=jnp.int32)[None, None, :, None]
    return inverse[group_ids, shifted].astype(jnp.int32)


def draw_adj_cols(key, part):
    return pattern_parts(key)


def draw_adj_vals(key, part):
    columns = pattern_parts(key)
    value_key = jax.random.fold_in(key, 103)
    total_panels = GROUPS * MEMBERS
    row_panel = jnp.arange(GROUPS, dtype=jnp.int32)[None, :, None, None] * MEMBERS + jnp.arange(MEMBERS, dtype=jnp.int32)[:, None, None, None]
    col_panel = jnp.arange(GROUPS, dtype=jnp.int32)[None, None, :, None] * MEMBERS + columns
    row_panel = jnp.broadcast_to(row_panel, columns.shape)
    lower = jnp.minimum(row_panel, col_panel)
    upper = jnp.maximum(row_panel, col_panel)
    flipped = row_panel > col_panel
    same = row_panel == col_panel
    factor = (BLOCK * NNZ * GROUPS) ** (-0.5)

    def one_block(entry):
        low_id, high_id, flip, diag = entry
        block_key = jax.random.fold_in(value_key, low_id * total_panels + high_id)
        base = jax.random.normal(block_key, (BLOCK, BLOCK), jnp.float32)
        mirrored = (base + base.T) * 0.70710678
        chosen = jnp.where(diag, mirrored, jnp.where(flip, base.T, base))
        return (chosen * factor).astype(jnp.bfloat16)

    def one_member(entry):
        return jax.vmap(one_block)(entry)
    flat = (lower.reshape(MEMBERS, -1), upper.reshape(MEMBERS, -1), flipped.reshape(MEMBERS, -1), same.reshape(MEMBERS, -1))
    blocks = lax.map(one_member, flat)
    return blocks.reshape(MEMBERS, GROUPS, GROUPS, NNZ, BLOCK, BLOCK)


def levels(own_key, shape, cuts, smallest, top_value):
    factor_of = 1.0
    for dim, shards_of in cuts:
        heights = jax.random.uniform(jax.random.fold_in(jax.random.fold_in(own_key, 6), dim), (shards_of,), jnp.float32, smallest / len(cuts), top_value / len(cuts))
        factor_of = factor_of * jnp.repeat(jnp.exp(heights), shape[dim] // shards_of).reshape((-1,) + (1,) * (len(shape) - 1 - dim))
    return factor_of


def gaussian(key, shape, scale, most, cuts=(), kind=jnp.bfloat16):
    entries = scale * jax.random.normal(key, shape, jnp.float32)
    if cuts:
        entries = entries * levels(key, shape, cuts, -0.22, 0.18)
    return jnp.clip(entries, -most, most).astype(kind)


def setup_inputs(seed: int = 0) -> dict:
    key_list = jax.random.split(jax.random.key(seed), 7)
    features = gaussian(key_list[0], (NODES, WIDTH), 1.0, 6.0, ((0, 512),))
    weight = gaussian(key_list[1], (WIDTH, WIDTH), WIDTH ** -0.5, 0.375)
    bias = gaussian(key_list[2], (WIDTH,), 0.5, 3.0, (), jnp.float32)
    cotangent = gaussian(key_list[3], (NODES, WIDTH), 1.0, 6.0, ((0, 512),))
    adj_cols = draw_adj_cols(jax.random.fold_in(key_list[6], 71), 0)
    adj_vals = draw_adj_vals(jax.random.fold_in(key_list[6], 71), 0)
    return {"features": features, "weight": weight, "bias": bias, "cotangent": cotangent, "adj_cols": adj_cols, "adj_vals": adj_vals}


def forward_rows(adj_vals, adj_cols, source):
    block = adj_vals.shape[-1]
    width = source.shape[1]
    panels = source.reshape(GROUPS, MEMBERS, block, width)
    group_ids = jnp.arange(GROUPS, dtype=jnp.int32)

    def one_member(pair):
        columns, values = pair
        picked = panels[group_ids[None, :, None], columns]
        return jnp.einsum('rbkij,rbkjf->rif', values.astype(jnp.float32), picked.astype(jnp.float32))
    result = lax.map(one_member, (adj_cols, adj_vals))
    return jnp.transpose(result, (1, 0, 2, 3)).reshape(-1, width)

def backward_rows(adj_vals, adj_cols, source):
    block = adj_vals.shape[-1]
    width = source.shape[1]
    panels = source.reshape(GROUPS, MEMBERS, block, width).astype(jnp.float32)
    group_ids = jnp.arange(GROUPS, dtype=jnp.int32)

    def one_member(total, member):
        columns = adj_cols[member]
        values = adj_vals[member].astype(jnp.float32)
        rows_here = panels[:, member]
        contrib = jnp.einsum('rbkij,rif->rbkjf', values, rows_here)
        total = total.at[group_ids[None, :, None], columns].add(contrib)
        return (total, None)
    start = jnp.zeros((GROUPS, MEMBERS, block, width), jnp.float32)
    total, unused = lax.scan(one_member, start, jnp.arange(MEMBERS, dtype=jnp.int32))
    return total.reshape(-1, width)

def activation(value):
    return jax.nn.gelu(value, approximate=True)

def reference(features, weight, bias, cotangent, adj_cols, adj_vals):
    product = jnp.dot(features, weight, preferred_element_type=jnp.float32).astype(jnp.bfloat16)
    summed = forward_rows(adj_vals, adj_cols, product)
    pre = summed + bias.astype(jnp.float32)[None, :]
    activated, pullback = jax.vjp(activation, pre)
    hidden = activated.astype(jnp.bfloat16)
    pulled = pullback(cotangent.astype(jnp.float32))[0].astype(jnp.bfloat16)
    spread = backward_rows(adj_vals, adj_cols, pulled).astype(jnp.bfloat16)
    grad_input = jnp.dot(spread, weight.T, preferred_element_type=jnp.float32).astype(jnp.bfloat16)
    grad_weight = lax.dot_general(features, spread, (((0,), (0,)), ((), ())), preferred_element_type=jnp.float32)
    grad_bias = lax.optimization_barrier(jnp.sum(pulled.astype(jnp.float32), axis=0))
    return (hidden, grad_input, grad_weight, grad_bias)
```

```python
import jax
import jax.numpy as jnp
from jax import lax
from jax.sharding import Mesh
from jax.sharding import PartitionSpec as P

BLK_AXES = ("y_lo", "core")
TEAM_AXES = ("y_hi", "x", "z")
PLANE = ("x", "z")
ALL_AXES = BLK_AXES + TEAM_AXES


def fine_mesh(mesh):
    blk = mesh.shape["blk"]
    team = mesh.shape["team"]
    sizes = (blk // 2, 2, 2, 4, team // 8)
    return Mesh(mesh.devices.reshape(sizes), ALL_AXES)


def gather_team(rows):
    other = lax.ppermute(rows, "y_hi", perm=[(0, 1), (1, 0)])
    pair = jnp.stack([rows, other], axis=0)
    full = lax.all_gather(pair, PLANE, axis=0, tiled=True)
    return full.reshape(-1, rows.shape[1])


def member_slots(members, plane_size):
    my_hi = lax.axis_index("y_hi")
    return (members % plane_size) * 2 + (members // plane_size != my_hi).astype(jnp.int32)


def collect(panels, slots, adj_vals):
    block = adj_vals.shape[-1]
    width = panels.shape[1]
    stacked = panels.reshape(panels.shape[0] // block, block, width)
    picked = jnp.take(stacked, slots, axis=0)
    summed = jnp.einsum(
        "rkij,rkjf->rif", adj_vals[0, :, 0], picked, preferred_element_type=jnp.float32
    )
    return summed.reshape(-1, width)


def activation(value):
    return jax.nn.gelu(value, approximate=True)


def local(features, weight, bias, cotangent, adj_cols, adj_vals):
    plane_size = lax.psum(1, PLANE)
    slots = member_slots(adj_cols[0, :, 0, :], plane_size)
    product = jnp.dot(features, weight, preferred_element_type=jnp.float32).astype(jnp.bfloat16)
    gathered = gather_team(product)
    partial_rows = collect(gathered, slots, adj_vals)
    summed = lax.psum_scatter(partial_rows, BLK_AXES, scatter_dimension=0, tiled=True)
    pre = summed + bias[None, :]
    activated, pullback = jax.vjp(activation, pre)
    hidden = activated.astype(jnp.bfloat16)
    pulled = pullback(cotangent.astype(jnp.float32))[0].astype(jnp.bfloat16)
    pulled_group = gather_team(pulled)
    partial_back = collect(pulled_group, slots, adj_vals)
    spread = lax.psum_scatter(partial_back, BLK_AXES, scatter_dimension=0, tiled=True).astype(
        jnp.bfloat16
    )
    grad_input = jnp.dot(spread, weight.T, preferred_element_type=jnp.float32).astype(jnp.bfloat16)
    local_weight = lax.dot_general(
        features, spread, (((0,), (0,)), ((), ())), preferred_element_type=jnp.float32
    )
    local_bias = jnp.sum(pulled.astype(jnp.float32), axis=0)
    both = jnp.concatenate([local_weight, local_bias[None, :]], axis=0)
    both = lax.psum(both, PLANE)
    both = lax.psum(both, ("y_lo", "y_hi", "core"))
    grad_weight = both[:-1]
    grad_bias = both[-1]
    return (hidden, grad_input, grad_weight, grad_bias)


def solution(mesh):
    fine = fine_mesh(mesh)
    rows = P(ALL_AXES, None)
    return jax.shard_map(
        local,
        mesh=fine,
        in_specs=(
            rows,
            P(),
            P(),
            rows,
            P(TEAM_AXES, None, BLK_AXES, None),
            P(TEAM_AXES, None, BLK_AXES, None, None, None),
        ),
        out_specs=(rows, rows, P(), P()),
        check_vma=False,
    )
```

```python
import jax
import jax.numpy as jnp
from jax import lax
from jax.sharding import Mesh
from jax.sharding import PartitionSpec as P

BLK_AXES = ("y_lo", "core")
TEAM_AXES = ("y_hi", "x", "z")
ALL_AXES = BLK_AXES + TEAM_AXES
SIZES = {}


def fine_mesh(mesh):
    blk = mesh.shape["blk"]
    team = mesh.shape["team"]
    sizes = (blk // 2, 2, 2, 4, team // 8)
    SIZES.update(zip(ALL_AXES, sizes))
    return Mesh(mesh.devices.reshape(sizes), ALL_AXES)


def ring_offsets(n):
    offsets = [0]
    for step in range(1, n // 2 + 1):
        offsets.append(-step)
        if step < n - step:
            offsets.append(step)
    return offsets


def ring_gather(blocks, axis):
    n = SIZES[axis]
    ahead = blocks
    behind = blocks
    parts = [blocks]
    for step in range(1, n // 2 + 1):
        ahead = lax.ppermute(ahead, axis, [(i, (i + 1) % n) for i in range(n)])
        parts.append(ahead)
        if step < n - step:
            behind = lax.ppermute(behind, axis, [(i, (i - 1) % n) for i in range(n)])
            parts.append(behind)
    return jnp.concatenate(parts, axis=0)


def gather_team(rows):
    other = lax.ppermute(rows, "y_hi", perm=[(0, 1), (1, 0)])
    pair = jnp.stack([rows, other], axis=0)
    full = ring_gather(ring_gather(pair, "x"), "z")
    return full.reshape(-1, rows.shape[1])


def ring_slot(delta, axis):
    n = SIZES[axis]
    order = [o % n for o in ring_offsets(n)]
    table = [order.index(d) for d in range(n)]
    return jnp.asarray(table, jnp.int32)[(delta + n) % n]


def member_slots(members):
    nx, nz = SIZES["x"], SIZES["z"]
    m_hi = members // (nx * nz)
    m_x = (members // nz) % nx
    m_z = members % nz
    y_slot = (m_hi != lax.axis_index("y_hi")).astype(jnp.int32)
    x_slot = ring_slot(m_x - lax.axis_index("x"), "x")
    z_slot = ring_slot(m_z - lax.axis_index("z"), "z")
    return (z_slot * nx + x_slot) * 2 + y_slot


def swap(value, axis, bit):
    n = SIZES[axis]
    return lax.ppermute(value, axis, [(i, i ^ bit) for i in range(n)])


BUTTERFLY = (("y_lo", 1), ("x", 1), ("z", 1), ("y_lo", 2), ("x", 2), ("z", 2), ("z", 4), ("y_hi", 1))


def all_sum(value):
    half = value.shape[0] // 2
    upper = lax.axis_index("core") == 1
    low, high = value[:half], value[half:]
    keep = jnp.where(upper, high, low)
    send = jnp.where(upper, low, high)
    part = keep + swap(send, "core", 1)
    for axis, bit in BUTTERFLY:
        if bit < SIZES[axis]:
            part = part + swap(part, axis, bit)
    other = swap(part, "core", 1)
    return jnp.where(upper, jnp.concatenate([other, part]), jnp.concatenate([part, other]))


def collect(panels, slots, adj_vals):
    block = adj_vals.shape[-1]
    width = panels.shape[1]
    stacked = panels.reshape(panels.shape[0] // block, block, width)
    picked = jnp.take(stacked, slots, axis=0)
    summed = jnp.einsum(
        "rkij,rkjf->rif", adj_vals[0, :, 0], picked, preferred_element_type=jnp.float32
    )
    return summed.reshape(-1, width)


def activation(value):
    return jax.nn.gelu(value, approximate=True)


def local(features, weight, bias, cotangent, adj_cols, adj_vals):
    slots = member_slots(adj_cols[0, :, 0, :])
    product = jnp.dot(features, weight, preferred_element_type=jnp.float32).astype(jnp.bfloat16)
    gathered = gather_team(product)
    partial_rows = collect(gathered, slots, adj_vals)
    summed = lax.psum_scatter(partial_rows, BLK_AXES, scatter_dimension=0, tiled=True)
    pre = summed + bias[None, :]
    activated, pullback = jax.vjp(activation, pre)
    hidden = activated.astype(jnp.bfloat16)
    pulled = pullback(cotangent.astype(jnp.float32))[0].astype(jnp.bfloat16)
    pulled_group = gather_team(pulled)
    partial_back = collect(pulled_group, slots, adj_vals)
    spread = lax.psum_scatter(partial_back, BLK_AXES, scatter_dimension=0, tiled=True).astype(
        jnp.bfloat16
    )
    grad_input = jnp.dot(spread, weight.T, preferred_element_type=jnp.float32).astype(jnp.bfloat16)
    local_weight = lax.dot_general(
        features, spread, (((0,), (0,)), ((), ())), preferred_element_type=jnp.float32
    )
    local_bias = jnp.sum(pulled.astype(jnp.float32), axis=0)
    width = local_weight.shape[0]
    filler = jnp.zeros((7, local_bias.shape[0]), jnp.float32)
    both = all_sum(jnp.concatenate([local_weight, local_bias[None, :], filler], axis=0))
    return (hidden, grad_input, both[:width], both[width])


def solution(mesh):
    fine = fine_mesh(mesh)
    rows = P(ALL_AXES, None)
    return jax.shard_map(
        local,
        mesh=fine,
        in_specs=(
            rows,
            P(),
            P(),
            rows,
            P(TEAM_AXES, None, BLK_AXES, None),
            P(TEAM_AXES, None, BLK_AXES, None, None, None),
        ),
        out_specs=(rows, rows, P(), P()),
        check_vma=False,
    )
```

```python
import jax
import jax.numpy as jnp
from jax import lax
from jax.sharding import Mesh
from jax.sharding import PartitionSpec as P

BLK_AXES = ("y_lo", "core")
TEAM_AXES = ("y_hi", "x", "z")
ALL_AXES = BLK_AXES + TEAM_AXES
SIZES = {}


def fine_mesh(mesh):
    blk = mesh.shape["blk"]
    team = mesh.shape["team"]
    sizes = (blk // 2, 2, 2, 4, team // 8)
    SIZES.update(zip(ALL_AXES, sizes))
    return Mesh(mesh.devices.reshape(sizes), ALL_AXES)


def ring_offsets(n):
    offsets = [0]
    for step in range(1, n // 2 + 1):
        offsets.append(-step)
        if step < n - step:
            offsets.append(step)
    return offsets


def ring_gather(blocks, axis):
    n = SIZES[axis]
    ahead = blocks
    behind = blocks
    parts = [blocks]
    for step in range(1, n // 2 + 1):
        ahead = lax.ppermute(ahead, axis, [(i, (i + 1) % n) for i in range(n)])
        parts.append(ahead)
        if step < n - step:
            behind = lax.ppermute(behind, axis, [(i, (i - 1) % n) for i in range(n)])
            parts.append(behind)
    return jnp.concatenate(parts, axis=0)


def gather_team(rows):
    other = lax.ppermute(rows, "y_hi", perm=[(0, 1), (1, 0)])
    pair = jnp.stack([rows, other], axis=0)
    full = ring_gather(ring_gather(pair, "x"), "z")
    return full.reshape(-1, rows.shape[1])


def ring_slot(delta, axis):
    n = SIZES[axis]
    order = [o % n for o in ring_offsets(n)]
    table = [order.index(d) for d in range(n)]
    return jnp.asarray(table, jnp.int32)[(delta + n) % n]


def member_slots(members):
    nx, nz = SIZES["x"], SIZES["z"]
    m_hi = members // (nx * nz)
    m_x = (members // nz) % nx
    m_z = members % nz
    y_slot = (m_hi != lax.axis_index("y_hi")).astype(jnp.int32)
    x_slot = ring_slot(m_x - lax.axis_index("x"), "x")
    z_slot = ring_slot(m_z - lax.axis_index("z"), "z")
    return (z_slot * nx + x_slot) * 2 + y_slot


def swap(value, axis, bit):
    n = SIZES[axis]
    return lax.ppermute(value, axis, [(i, i ^ bit) for i in range(n)])


BUTTERFLY = (("y_lo", 1), ("x", 1), ("z", 1), ("y_lo", 2), ("x", 2), ("z", 2), ("z", 4), ("y_hi", 1))


def all_sum(value):
    half = value.shape[0] // 2
    upper = lax.axis_index("core") == 1
    low, high = value[:half], value[half:]
    keep = jnp.where(upper, high, low)
    send = jnp.where(upper, low, high)
    part = keep + swap(send, "core", 1)
    for axis, bit in BUTTERFLY:
        if bit < SIZES[axis]:
            part = part + swap(part, axis, bit)
    other = swap(part, "core", 1)
    return jnp.where(upper, jnp.concatenate([other, part]), jnp.concatenate([part, other]))


def blk_reduce_scatter(partial):
    width = partial.shape[-1]
    block = partial.shape[0] // (SIZES["y_lo"] * SIZES["core"])
    cur = partial.reshape(-1, 2, block, width)
    upper = lax.axis_index("core") == 1
    keep = jnp.where(upper, cur[:, 1], cur[:, 0])
    send = jnp.where(upper, cur[:, 0], cur[:, 1])
    cur = keep + swap(send, "core", 1)
    bit = 1
    while bit < SIZES["y_lo"]:
        cur = cur.reshape(-1, 2, block, width)
        upper = (lax.axis_index("y_lo") & bit) != 0
        keep = jnp.where(upper, cur[:, 1], cur[:, 0])
        send = jnp.where(upper, cur[:, 0], cur[:, 1])
        cur = keep + swap(send, "y_lo", bit)
        bit *= 2
    return cur.reshape(block, width)


def collect(panels, slots, adj_vals):
    block = adj_vals.shape[-1]
    width = panels.shape[1]
    stacked = panels.reshape(panels.shape[0] // block, block, width)
    picked = jnp.take(stacked, slots, axis=0)
    summed = jnp.einsum(
        "rkij,rkjf->rif", adj_vals[0, :, 0], picked, preferred_element_type=jnp.float32
    )
    return summed.reshape(-1, width)


def activation(value):
    return jax.nn.gelu(value, approximate=True)


def local(features, weight, bias, cotangent, adj_cols, adj_vals):
    slots = member_slots(adj_cols[0, :, 0, :])
    product = jnp.dot(features, weight, preferred_element_type=jnp.float32).astype(jnp.bfloat16)
    gathered = gather_team(product)
    partial_rows = collect(gathered, slots, adj_vals)
    summed = blk_reduce_scatter(partial_rows)
    pre = summed + bias[None, :]
    activated, pullback = jax.vjp(activation, pre)
    hidden = activated.astype(jnp.bfloat16)
    pulled = pullback(cotangent.astype(jnp.float32))[0].astype(jnp.bfloat16)
    pulled_group = gather_team(pulled)
    partial_back = collect(pulled_group, slots, adj_vals)
    spread = blk_reduce_scatter(partial_back).astype(jnp.bfloat16)
    grad_input = jnp.dot(spread, weight.T, preferred_element_type=jnp.float32).astype(jnp.bfloat16)
    local_weight = lax.dot_general(
        features, spread, (((0,), (0,)), ((), ())), preferred_element_type=jnp.float32
    )
    local_bias = jnp.sum(pulled.astype(jnp.float32), axis=0)
    width = local_weight.shape[0]
    filler = jnp.zeros((7, local_bias.shape[0]), jnp.float32)
    both = all_sum(jnp.concatenate([local_weight, local_bias[None, :], filler], axis=0))
    return (hidden, grad_input, both[:width], both[width])


def solution(mesh):
    fine = fine_mesh(mesh)
    rows = P(ALL_AXES, None)
    return jax.shard_map(
        local,
        mesh=fine,
        in_specs=(
            rows,
            P(),
            P(),
            rows,
            P(TEAM_AXES, None, BLK_AXES, None),
            P(TEAM_AXES, None, BLK_AXES, None, None, None),
        ),
        out_specs=(rows, rows, P(), P()),
        check_vma=False,
    )
```

```python
import jax
import jax.numpy as jnp
from jax import lax
from jax.sharding import Mesh
from jax.sharding import PartitionSpec as P

BLK_AXES = ("y_lo", "core")
TEAM_AXES = ("y_hi", "x", "z")
ALL_AXES = BLK_AXES + TEAM_AXES
SIZES = {}


def fine_mesh(mesh):
    blk = mesh.shape["blk"]
    team = mesh.shape["team"]
    sizes = (blk // 2, 2, 2, 4, team // 8)
    SIZES.update(zip(ALL_AXES, sizes))
    return Mesh(mesh.devices.reshape(sizes), ALL_AXES)


def ring_offsets(n):
    offsets = [0]
    for step in range(1, n // 2 + 1):
        offsets.append(-step)
        if step < n - step:
            offsets.append(step)
    return offsets


def ring_gather(blocks, axis):
    n = SIZES[axis]
    ahead = blocks
    behind = blocks
    parts = [blocks]
    for step in range(1, n // 2 + 1):
        ahead = lax.ppermute(ahead, axis, [(i, (i + 1) % n) for i in range(n)])
        parts.append(ahead)
        if step < n - step:
            behind = lax.ppermute(behind, axis, [(i, (i - 1) % n) for i in range(n)])
            parts.append(behind)
    return jnp.concatenate(parts, axis=0)


def gather_team(rows):
    other = lax.ppermute(rows, "y_hi", perm=[(0, 1), (1, 0)])
    pair = jnp.stack([rows, other], axis=0)
    full = ring_gather(ring_gather(pair, "x"), "z")
    return full.reshape(-1, rows.shape[1])


def ring_slot(delta, axis):
    n = SIZES[axis]
    order = [o % n for o in ring_offsets(n)]
    table = [order.index(d) for d in range(n)]
    return jnp.asarray(table, jnp.int32)[(delta + n) % n]


def member_slots(members):
    nx, nz = SIZES["x"], SIZES["z"]
    m_hi = members // (nx * nz)
    m_x = (members // nz) % nx
    m_z = members % nz
    y_slot = (m_hi != lax.axis_index("y_hi")).astype(jnp.int32)
    x_slot = ring_slot(m_x - lax.axis_index("x"), "x")
    z_slot = ring_slot(m_z - lax.axis_index("z"), "z")
    return (z_slot * nx + x_slot) * 2 + y_slot


def swap(value, axis, bit):
    n = SIZES[axis]
    return lax.ppermute(value, axis, [(i, i ^ bit) for i in range(n)])


BUTTERFLY = (("y_lo", 1), ("x", 1), ("z", 1), ("y_lo", 2), ("x", 2), ("z", 2), ("z", 4), ("y_hi", 1))


def all_sum(value):
    half = value.shape[0] // 2
    upper = lax.axis_index("core") == 1
    low, high = value[:half], value[half:]
    keep = jnp.where(upper, high, low)
    send = jnp.where(upper, low, high)
    part = keep + swap(send, "core", 1)
    for axis, bit in BUTTERFLY:
        if bit < SIZES[axis]:
            part = part + swap(part, axis, bit)
    other = swap(part, "core", 1)
    return jnp.where(upper, jnp.concatenate([other, part]), jnp.concatenate([part, other]))


def blk_reduce_scatter(partial):
    width = partial.shape[-1]
    block = partial.shape[0] // (SIZES["y_lo"] * SIZES["core"])
    cur = partial.reshape(-1, 2, block, width)
    upper = lax.axis_index("core") == 1
    keep = jnp.where(upper, cur[:, 1], cur[:, 0])
    send = jnp.where(upper, cur[:, 0], cur[:, 1])
    cur = keep + swap(send, "core", 1)
    bit = 1
    while bit < SIZES["y_lo"]:
        cur = cur.reshape(-1, 2, block, width)
        upper = (lax.axis_index("y_lo") & bit) != 0
        keep = jnp.where(upper, cur[:, 1], cur[:, 0])
        send = jnp.where(upper, cur[:, 0], cur[:, 1])
        cur = keep + swap(send, "y_lo", bit)
        bit *= 2
    return cur.reshape(block, width)


def collect(panels, slots, adj_vals):
    block = adj_vals.shape[-1]
    width = panels.shape[1]
    stacked = panels.reshape(panels.shape[0] // block, block, width)
    picked = jnp.take(stacked, slots, axis=0)
    summed = jnp.einsum(
        "rkij,rkjf->rif", adj_vals[0, :, 0], picked, preferred_element_type=jnp.float32
    )
    return summed.reshape(-1, width)


def activation(value):
    return jax.nn.gelu(value, approximate=True)


def local(features, weight, bias, cotangent, adj_cols, adj_vals):
    slots = member_slots(adj_cols[0, :, 0, :])
    width = features.shape[1]
    block = adj_vals.shape[-1]
    gathered = gather_team(features)
    products = jnp.dot(gathered, weight, preferred_element_type=jnp.float32).astype(jnp.bfloat16)
    partial_rows = collect(products, slots, adj_vals)
    partial_ax = collect(gathered, slots, adj_vals)
    summed = blk_reduce_scatter(partial_rows)
    pre = summed + bias[None, :]
    activated, pullback = jax.vjp(activation, pre)
    hidden = activated.astype(jnp.bfloat16)
    pulled = pullback(cotangent.astype(jnp.float32))[0].astype(jnp.bfloat16)
    pulled_rows = lax.all_gather(pulled, BLK_AXES, axis=0, tiled=False)
    local_weight = jnp.einsum(
        "rnf,rng->fg",
        partial_ax.reshape(-1, block, width),
        pulled_rows.astype(jnp.float32),
        precision=lax.Precision.HIGHEST,
        preferred_element_type=jnp.float32,
    )
    local_bias = jnp.sum(pulled.astype(jnp.float32), axis=0)
    filler = jnp.zeros((7, local_bias.shape[0]), jnp.float32)
    both = all_sum(jnp.concatenate([local_weight, local_bias[None, :], filler], axis=0))
    pulled_group = gather_team(pulled)
    partial_back = collect(pulled_group, slots, adj_vals)
    spread = blk_reduce_scatter(partial_back).astype(jnp.bfloat16)
    grad_input = jnp.dot(spread, weight.T, preferred_element_type=jnp.float32).astype(jnp.bfloat16)
    return (hidden, grad_input, both[:width], both[width])


def solution(mesh):
    fine = fine_mesh(mesh)
    rows = P(ALL_AXES, None)
    return jax.shard_map(
        local,
        mesh=fine,
        in_specs=(
            rows,
            P(),
            P(),
            rows,
            P(TEAM_AXES, None, BLK_AXES, None),
            P(TEAM_AXES, None, BLK_AXES, None, None, None),
        ),
        out_specs=(rows, rows, P(), P()),
        check_vma=False,
    )
```

```python
import jax
import jax.numpy as jnp
from jax import lax
from jax.experimental import pallas as pl
from jax.experimental.pallas import tpu as pltpu
from jax.sharding import Mesh
from jax.sharding import PartitionSpec as P

BLK_AXES = ("y_lo", "core")
TEAM_AXES = ("y_hi", "x", "z")
ALL_AXES = BLK_AXES + TEAM_AXES
SIZES = {}


def fine_mesh(mesh):
    blk = mesh.shape["blk"]
    team = mesh.shape["team"]
    sizes = (blk // 2, 2, 2, 4, team // 8)
    SIZES.update(zip(ALL_AXES, sizes))
    return Mesh(mesh.devices.reshape(sizes), ALL_AXES)


def ring_offsets(n):
    offsets = [0]
    for step in range(1, n // 2 + 1):
        offsets.append(-step)
        if step < n - step:
            offsets.append(step)
    return offsets


def ring_gather(blocks, axis):
    n = SIZES[axis]
    ahead = blocks
    behind = blocks
    parts = [blocks]
    for step in range(1, n // 2 + 1):
        ahead = lax.ppermute(ahead, axis, [(i, (i + 1) % n) for i in range(n)])
        parts.append(ahead)
        if step < n - step:
            behind = lax.ppermute(behind, axis, [(i, (i - 1) % n) for i in range(n)])
            parts.append(behind)
    return jnp.concatenate(parts, axis=0)


def gather_team(rows):
    other = lax.ppermute(rows, "y_hi", perm=[(0, 1), (1, 0)])
    pair = jnp.stack([rows, other], axis=0)
    full = ring_gather(ring_gather(pair, "x"), "z")
    return full.reshape(-1, rows.shape[1])


def ring_slot(delta, axis):
    n = SIZES[axis]
    order = [o % n for o in ring_offsets(n)]
    table = [order.index(d) for d in range(n)]
    return jnp.asarray(table, jnp.int32)[(delta + n) % n]


def member_slots(members):
    nx, nz = SIZES["x"], SIZES["z"]
    m_hi = members // (nx * nz)
    m_x = (members // nz) % nx
    m_z = members % nz
    y_slot = (m_hi != lax.axis_index("y_hi")).astype(jnp.int32)
    x_slot = ring_slot(m_x - lax.axis_index("x"), "x")
    z_slot = ring_slot(m_z - lax.axis_index("z"), "z")
    return (z_slot * nx + x_slot) * 2 + y_slot


def swap(value, axis, bit):
    n = SIZES[axis]
    return lax.ppermute(value, axis, [(i, i ^ bit) for i in range(n)])


BUTTERFLY = (("y_lo", 1), ("x", 1), ("z", 1), ("y_lo", 2), ("x", 2), ("z", 2), ("z", 4), ("y_hi", 1))


def all_sum(value):
    half = value.shape[0] // 2
    upper = lax.axis_index("core") == 1
    low, high = value[:half], value[half:]
    keep = jnp.where(upper, high, low)
    send = jnp.where(upper, low, high)
    part = keep + swap(send, "core", 1)
    for axis, bit in BUTTERFLY:
        if bit < SIZES[axis]:
            part = part + swap(part, axis, bit)
    other = swap(part, "core", 1)
    return jnp.where(upper, jnp.concatenate([other, part]), jnp.concatenate([part, other]))


def blk_reduce_scatter(partial):
    width = partial.shape[-1]
    block = partial.shape[0] // (SIZES["y_lo"] * SIZES["core"])
    cur = partial.reshape(-1, 2, block, width)
    upper = lax.axis_index("core") == 1
    keep = jnp.where(upper, cur[:, 1], cur[:, 0])
    send = jnp.where(upper, cur[:, 0], cur[:, 1])
    cur = keep + swap(send, "core", 1)
    bit = 1
    while bit < SIZES["y_lo"]:
        cur = cur.reshape(-1, 2, block, width)
        upper = (lax.axis_index("y_lo") & bit) != 0
        keep = jnp.where(upper, cur[:, 1], cur[:, 0])
        send = jnp.where(upper, cur[:, 0], cur[:, 1])
        cur = keep + swap(send, "y_lo", bit)
        bit *= 2
    return cur.reshape(block, width)


def collect_kernel(slots_ref, vals_ref, panels_ref, out_ref):
    row = pl.program_id(0)
    nnz = vals_ref.shape[0]
    total = jnp.zeros(out_ref.shape, jnp.float32)
    for k in range(nnz):
        slot = slots_ref[row * nnz + k]
        total = total + jnp.dot(vals_ref[k], panels_ref[slot], preferred_element_type=jnp.float32)
    out_ref[...] = total


def collect(panels, slots, adj_vals):
    block = adj_vals.shape[-1]
    width = panels.shape[1]
    rows, nnz = slots.shape
    stacked = panels.reshape(panels.shape[0] // block, block, width)
    grid_spec = pltpu.PrefetchScalarGridSpec(
        num_scalar_prefetch=1,
        grid=(rows,),
        in_specs=[
            pl.BlockSpec((None, None, None, nnz, block, block), lambda r, s: (0, r, 0, 0, 0, 0)),
            pl.BlockSpec(stacked.shape, lambda r, s: (0, 0, 0)),
        ],
        out_specs=pl.BlockSpec((block, width), lambda r, s: (r, 0)),
    )
    return pl.pallas_call(
        collect_kernel,
        grid_spec=grid_spec,
        out_shape=jax.ShapeDtypeStruct((rows * block, width), jnp.float32),
        cost_estimate=pl.CostEstimate(
            flops=2 * rows * nnz * block * block * width,
            transcendentals=0,
            bytes_accessed=stacked.size * 2 + rows * nnz * block * block * 2 + rows * block * width * 4,
        ),
    )(slots.reshape(-1), adj_vals, stacked)


def activation(value):
    return jax.nn.gelu(value, approximate=True)


def local(features, weight, bias, cotangent, adj_cols, adj_vals):
    slots = member_slots(adj_cols[0, :, 0, :])
    product = jnp.dot(features, weight, preferred_element_type=jnp.float32).astype(jnp.bfloat16)
    gathered = gather_team(product)
    partial_rows = collect(gathered, slots, adj_vals)
    summed = blk_reduce_scatter(partial_rows)
    pre = summed + bias[None, :]
    activated, pullback = jax.vjp(activation, pre)
    hidden = activated.astype(jnp.bfloat16)
    pulled = pullback(cotangent.astype(jnp.float32))[0].astype(jnp.bfloat16)
    pulled_group = gather_team(pulled)
    partial_back = collect(pulled_group, slots, adj_vals)
    spread = blk_reduce_scatter(partial_back).astype(jnp.bfloat16)
    grad_input = jnp.dot(spread, weight.T, preferred_element_type=jnp.float32).astype(jnp.bfloat16)
    local_weight = lax.dot_general(
        features, spread, (((0,), (0,)), ((), ())), preferred_element_type=jnp.float32
    )
    local_bias = jnp.sum(pulled.astype(jnp.float32), axis=0)
    width = local_weight.shape[0]
    filler = jnp.zeros((7, local_bias.shape[0]), jnp.float32)
    both = all_sum(jnp.concatenate([local_weight, local_bias[None, :], filler], axis=0))
    return (hidden, grad_input, both[:width], both[width])


def solution(mesh):
    fine = fine_mesh(mesh)
    rows = P(ALL_AXES, None)
    return jax.shard_map(
        local,
        mesh=fine,
        in_specs=(
            rows,
            P(),
            P(),
            rows,
            P(TEAM_AXES, None, BLK_AXES, None),
            P(TEAM_AXES, None, BLK_AXES, None, None, None),
        ),
        out_specs=(rows, rows, P(), P()),
        check_vma=False,
    )
```

```python
import jax
import jax.numpy as jnp
from jax import lax
from jax.experimental import pallas as pl
from jax.experimental.pallas import tpu as pltpu
from jax.sharding import Mesh
from jax.sharding import PartitionSpec as P

BLK_AXES = ("y_lo", "core")
TEAM_AXES = ("y_hi", "x", "z")
ALL_AXES = BLK_AXES + TEAM_AXES
SIZES = {}


def fine_mesh(mesh):
    blk = mesh.shape["blk"]
    team = mesh.shape["team"]
    sizes = (blk // 2, 2, 2, 4, team // 8)
    SIZES.update(zip(ALL_AXES, sizes))
    return Mesh(mesh.devices.reshape(sizes), ALL_AXES)


def ring_offsets(n):
    offsets = [0]
    for step in range(1, n // 2 + 1):
        offsets.append(-step)
        if step < n - step:
            offsets.append(step)
    return offsets


def ring_gather(blocks, axis):
    n = SIZES[axis]
    ahead = blocks
    behind = blocks
    parts = [blocks]
    for step in range(1, n // 2 + 1):
        ahead = lax.ppermute(ahead, axis, [(i, (i + 1) % n) for i in range(n)])
        parts.append(ahead)
        if step < n - step:
            behind = lax.ppermute(behind, axis, [(i, (i - 1) % n) for i in range(n)])
            parts.append(behind)
    return jnp.concatenate(parts, axis=0)


def gather_team(rows):
    other = lax.ppermute(rows, "y_hi", perm=[(0, 1), (1, 0)])
    pair = jnp.stack([rows, other], axis=0)
    full = ring_gather(ring_gather(pair, "x"), "z")
    return full.reshape(-1, rows.shape[1])


def ring_slot(delta, axis):
    n = SIZES[axis]
    order = [o % n for o in ring_offsets(n)]
    table = [order.index(d) for d in range(n)]
    return jnp.asarray(table, jnp.int32)[(delta + n) % n]


def member_slots(members):
    nx, nz = SIZES["x"], SIZES["z"]
    m_hi = members // (nx * nz)
    m_x = (members // nz) % nx
    m_z = members % nz
    y_slot = (m_hi != lax.axis_index("y_hi")).astype(jnp.int32)
    x_slot = ring_slot(m_x - lax.axis_index("x"), "x")
    z_slot = ring_slot(m_z - lax.axis_index("z"), "z")
    return (z_slot * nx + x_slot) * 2 + y_slot


def swap(value, axis, bit):
    n = SIZES[axis]
    return lax.ppermute(value, axis, [(i, i ^ bit) for i in range(n)])


BUTTERFLY = (("y_lo", 1), ("x", 1), ("z", 1), ("y_lo", 2), ("x", 2), ("z", 2), ("z", 4), ("y_hi", 1))


def all_sum(value):
    half = value.shape[0] // 2
    upper = lax.axis_index("core") == 1
    low, high = value[:half], value[half:]
    keep = jnp.where(upper, high, low)
    send = jnp.where(upper, low, high)
    part = keep + swap(send, "core", 1)
    for axis, bit in BUTTERFLY:
        if bit < SIZES[axis]:
            part = part + swap(part, axis, bit)
    other = swap(part, "core", 1)
    return jnp.where(upper, jnp.concatenate([other, part]), jnp.concatenate([part, other]))


def blk_reduce_scatter(partial):
    width = partial.shape[-1]
    block = partial.shape[0] // (SIZES["y_lo"] * SIZES["core"])
    cur = partial.reshape(-1, 2, block, width)
    upper = lax.axis_index("core") == 1
    keep = jnp.where(upper, cur[:, 1], cur[:, 0])
    send = jnp.where(upper, cur[:, 0], cur[:, 1])
    cur = keep + swap(send, "core", 1)
    bit = 1
    while bit < SIZES["y_lo"]:
        cur = cur.reshape(-1, 2, block, width)
        upper = (lax.axis_index("y_lo") & bit) != 0
        keep = jnp.where(upper, cur[:, 1], cur[:, 0])
        send = jnp.where(upper, cur[:, 0], cur[:, 1])
        cur = keep + swap(send, "y_lo", bit)
        bit *= 2
    return cur.reshape(block, width)


def blk_all_gather(rows):
    cur = rows[None]
    bit = 1
    while bit < SIZES["y_lo"]:
        upper = (lax.axis_index("y_lo") & bit) != 0
        got = swap(cur, "y_lo", bit)
        cur = jnp.where(upper, jnp.concatenate([got, cur]), jnp.concatenate([cur, got]))
        bit *= 2
    upper = lax.axis_index("core") == 1
    got = swap(cur, "core", 1)
    cur = jnp.where(upper, jnp.stack([got, cur], axis=1), jnp.stack([cur, got], axis=1))
    return cur.reshape((-1,) + rows.shape)


def collect_kernel(slots_ref, vals_ref, panels_ref, out_ref):
    row = pl.program_id(0)
    nnz = vals_ref.shape[0]
    total = jnp.zeros(out_ref.shape, jnp.float32)
    for k in range(nnz):
        slot = slots_ref[row * nnz + k]
        total = total + jnp.dot(vals_ref[k], panels_ref[slot], preferred_element_type=jnp.float32)
    out_ref[...] = total


def collect(panels, slots, adj_vals):
    block = adj_vals.shape[-1]
    width = panels.shape[1]
    rows, nnz = slots.shape
    stacked = panels.reshape(panels.shape[0] // block, block, width)
    grid_spec = pltpu.PrefetchScalarGridSpec(
        num_scalar_prefetch=1,
        grid=(rows,),
        in_specs=[
            pl.BlockSpec((None, None, None, nnz, block, block), lambda r, s: (0, r, 0, 0, 0, 0)),
            pl.BlockSpec(stacked.shape, lambda r, s: (0, 0, 0)),
        ],
        out_specs=pl.BlockSpec((block, width), lambda r, s: (r, 0)),
    )
    return pl.pallas_call(
        collect_kernel,
        grid_spec=grid_spec,
        out_shape=jax.ShapeDtypeStruct((rows * block, width), jnp.float32),
        cost_estimate=pl.CostEstimate(
            flops=2 * rows * nnz * block * block * width,
            transcendentals=0,
            bytes_accessed=stacked.size * 2 + rows * nnz * block * block * 2 + rows * block * width * 4,
        ),
    )(slots.reshape(-1), adj_vals, stacked)


def activation(value):
    return jax.nn.gelu(value, approximate=True)


def local(features, weight, bias, cotangent, adj_cols, adj_vals):
    slots = member_slots(adj_cols[0, :, 0, :])
    width = features.shape[1]
    gathered = gather_team(features)
    products = jnp.dot(gathered, weight, preferred_element_type=jnp.float32).astype(jnp.bfloat16)
    partial_rows = collect(products, slots, adj_vals)
    partial_ax = collect(gathered, slots, adj_vals)
    summed = blk_reduce_scatter(partial_rows)
    pre = summed + bias[None, :]
    activated, pullback = jax.vjp(activation, pre)
    hidden = activated.astype(jnp.bfloat16)
    pulled = pullback(cotangent.astype(jnp.float32))[0].astype(jnp.bfloat16)
    pulled_rows = blk_all_gather(pulled)
    local_weight = jnp.einsum(
        "rnf,rng->fg",
        partial_ax.reshape(pulled_rows.shape),
        pulled_rows.astype(jnp.float32),
        precision=lax.Precision.HIGHEST,
        preferred_element_type=jnp.float32,
    )
    local_bias = jnp.sum(pulled.astype(jnp.float32), axis=0)
    filler = jnp.zeros((7, local_bias.shape[0]), jnp.float32)
    both = all_sum(jnp.concatenate([local_weight, local_bias[None, :], filler], axis=0))
    pulled_group = gather_team(pulled)
    partial_back = collect(pulled_group, slots, adj_vals)
    spread = blk_reduce_scatter(partial_back).astype(jnp.bfloat16)
    grad_input = jnp.dot(spread, weight.T, preferred_element_type=jnp.float32).astype(jnp.bfloat16)
    return (hidden, grad_input, both[:width], both[width])


def solution(mesh):
    fine = fine_mesh(mesh)
    rows = P(ALL_AXES, None)
    return jax.shard_map(
        local,
        mesh=fine,
        in_specs=(
            rows,
            P(),
            P(),
            rows,
            P(TEAM_AXES, None, BLK_AXES, None),
            P(TEAM_AXES, None, BLK_AXES, None, None, None),
        ),
        out_specs=(rows, rows, P(), P()),
        check_vma=False,
    )
```

```python
import jax
import jax.numpy as jnp
from jax import lax
from jax.experimental import pallas as pl
from jax.experimental.pallas import tpu as pltpu
from jax.sharding import Mesh
from jax.sharding import PartitionSpec as P

BLK_AXES = ("y_lo", "core")
TEAM_AXES = ("y_hi", "x", "z")
ALL_AXES = BLK_AXES + TEAM_AXES
SIZES = {}


def fine_mesh(mesh):
    blk = mesh.shape["blk"]
    team = mesh.shape["team"]
    sizes = (blk // 2, 2, 2, 4, team // 8)
    SIZES.update(zip(ALL_AXES, sizes))
    return Mesh(mesh.devices.reshape(sizes), ALL_AXES)


def ring_offsets(n):
    offsets = [0]
    for step in range(1, n // 2 + 1):
        offsets.append(-step)
        if step < n - step:
            offsets.append(step)
    return offsets


def ring_gather(blocks, axis):
    n = SIZES[axis]
    ahead = blocks
    behind = blocks
    parts = [blocks]
    for step in range(1, n // 2 + 1):
        ahead = lax.ppermute(ahead, axis, [(i, (i + 1) % n) for i in range(n)])
        parts.append(ahead)
        if step < n - step:
            behind = lax.ppermute(behind, axis, [(i, (i - 1) % n) for i in range(n)])
            parts.append(behind)
    return jnp.concatenate(parts, axis=0)


def gather_team(rows):
    other = lax.ppermute(rows, "y_hi", perm=[(0, 1), (1, 0)])
    pair = jnp.stack([rows, other], axis=0)
    full = ring_gather(ring_gather(pair, "x"), "z")
    return full.reshape(-1, rows.shape[1])


def ring_slot(delta, axis):
    n = SIZES[axis]
    order = [o % n for o in ring_offsets(n)]
    table = [order.index(d) for d in range(n)]
    return jnp.asarray(table, jnp.int32)[(delta + n) % n]


def member_slots(members):
    nx, nz = SIZES["x"], SIZES["z"]
    m_hi = members // (nx * nz)
    m_x = (members // nz) % nx
    m_z = members % nz
    y_slot = (m_hi != lax.axis_index("y_hi")).astype(jnp.int32)
    x_slot = ring_slot(m_x - lax.axis_index("x"), "x")
    z_slot = ring_slot(m_z - lax.axis_index("z"), "z")
    return (z_slot * nx + x_slot) * 2 + y_slot


def swap(value, axis, bit):
    n = SIZES[axis]
    return lax.ppermute(value, axis, [(i, i ^ bit) for i in range(n)])


BUTTERFLY = (("y_lo", 1), ("x", 1), ("z", 1), ("y_lo", 2), ("x", 2), ("z", 2), ("z", 4), ("y_hi", 1))


def all_sum(value):
    half = value.shape[0] // 2
    upper = lax.axis_index("core") == 1
    low, high = value[:half], value[half:]
    keep = jnp.where(upper, high, low)
    send = jnp.where(upper, low, high)
    part = keep + swap(send, "core", 1)
    for axis, bit in BUTTERFLY:
        if bit < SIZES[axis]:
            part = part + swap(part, axis, bit)
    other = swap(part, "core", 1)
    return jnp.where(upper, jnp.concatenate([other, part]), jnp.concatenate([part, other]))


def blk_reduce_scatter(partial):
    width = partial.shape[-1]
    block = partial.shape[0] // (SIZES["y_lo"] * SIZES["core"])
    cur = partial.reshape(-1, 2, block, width)
    upper = lax.axis_index("core") == 1
    keep = jnp.where(upper, cur[:, 1], cur[:, 0])
    send = jnp.where(upper, cur[:, 0], cur[:, 1])
    cur = keep + swap(send, "core", 1)
    bit = 1
    while bit < SIZES["y_lo"]:
        cur = cur.reshape(-1, 2, block, width)
        upper = (lax.axis_index("y_lo") & bit) != 0
        keep = jnp.where(upper, cur[:, 1], cur[:, 0])
        send = jnp.where(upper, cur[:, 0], cur[:, 1])
        cur = keep + swap(send, "y_lo", bit)
        bit *= 2
    return cur.reshape(block, width)


def blk_all_gather(rows):
    cur = rows[None]
    bit = 1
    while bit < SIZES["y_lo"]:
        upper = (lax.axis_index("y_lo") & bit) != 0
        got = swap(cur, "y_lo", bit)
        cur = jnp.where(upper, jnp.concatenate([got, cur]), jnp.concatenate([cur, got]))
        bit *= 2
    upper = lax.axis_index("core") == 1
    got = swap(cur, "core", 1)
    cur = jnp.where(upper, jnp.stack([got, cur], axis=1), jnp.stack([cur, got], axis=1))
    return cur.reshape((-1,) + rows.shape)


def collect_kernel(slots_ref, vals_ref, panels_ref, out_ref):
    row = pl.program_id(0)
    nnz = vals_ref.shape[0]
    total = jnp.zeros(out_ref.shape, jnp.float32)
    for k in range(nnz):
        slot = slots_ref[row * nnz + k]
        total = total + jnp.dot(vals_ref[k], panels_ref[slot], preferred_element_type=jnp.float32)
    out_ref[...] = total


def collect(panels, slots, adj_vals):
    block = adj_vals.shape[-1]
    width = panels.shape[1]
    rows, nnz = slots.shape
    stacked = panels.reshape(panels.shape[0] // block, block, width)
    grid_spec = pltpu.PrefetchScalarGridSpec(
        num_scalar_prefetch=1,
        grid=(rows,),
        in_specs=[
            pl.BlockSpec((None, None, None, nnz, block, block), lambda r, s: (0, r, 0, 0, 0, 0)),
            pl.BlockSpec(stacked.shape, lambda r, s: (0, 0, 0)),
        ],
        out_specs=pl.BlockSpec((block, width), lambda r, s: (r, 0)),
    )
    return pl.pallas_call(
        collect_kernel,
        grid_spec=grid_spec,
        out_shape=jax.ShapeDtypeStruct((rows * block, width), jnp.float32),
        cost_estimate=pl.CostEstimate(
            flops=2 * rows * nnz * block * block * width,
            transcendentals=0,
            bytes_accessed=stacked.size * 2 + rows * nnz * block * block * 2 + rows * block * width * 4,
        ),
    )(slots.reshape(-1), adj_vals, stacked)


def activation(value):
    return jax.nn.gelu(value, approximate=True)


def local(features, weight, bias, cotangent, adj_cols, adj_vals):
    slots = member_slots(adj_cols[0, :, 0, :])
    width = features.shape[1]
    gathered = gather_team(features)
    partial_ax = collect(gathered, slots, adj_vals)
    partial_rows = jnp.dot(
        partial_ax,
        weight.astype(jnp.float32),
        precision=lax.Precision.HIGHEST,
        preferred_element_type=jnp.float32,
    )
    summed = blk_reduce_scatter(partial_rows)
    pre = summed + bias[None, :]
    activated, pullback = jax.vjp(activation, pre)
    hidden = activated.astype(jnp.bfloat16)
    pulled = pullback(cotangent.astype(jnp.float32))[0].astype(jnp.bfloat16)
    pulled_rows = blk_all_gather(pulled)
    local_weight = jnp.einsum(
        "rnf,rng->fg",
        partial_ax.reshape(pulled_rows.shape),
        pulled_rows.astype(jnp.float32),
        precision=lax.Precision.HIGHEST,
        preferred_element_type=jnp.float32,
    )
    local_bias = jnp.sum(pulled.astype(jnp.float32), axis=0)
    filler = jnp.zeros((7, local_bias.shape[0]), jnp.float32)
    both = all_sum(jnp.concatenate([local_weight, local_bias[None, :], filler], axis=0))
    pulled_group = gather_team(pulled)
    partial_back = collect(pulled_group, slots, adj_vals)
    spread = blk_reduce_scatter(partial_back).astype(jnp.bfloat16)
    grad_input = jnp.dot(spread, weight.T, preferred_element_type=jnp.float32).astype(jnp.bfloat16)
    return (hidden, grad_input, both[:width], both[width])


def solution(mesh):
    fine = fine_mesh(mesh)
    rows = P(ALL_AXES, None)
    return jax.shard_map(
        local,
        mesh=fine,
        in_specs=(
            rows,
            P(),
            P(),
            rows,
            P(TEAM_AXES, None, BLK_AXES, None),
            P(TEAM_AXES, None, BLK_AXES, None, None, None),
        ),
        out_specs=(rows, rows, P(), P()),
        check_vma=False,
    )
```

```python
import jax
import jax.numpy as jnp
from jax import lax
from jax.experimental import pallas as pl
from jax.experimental.pallas import tpu as pltpu
from jax.sharding import Mesh
from jax.sharding import PartitionSpec as P

BLK_AXES = ("y_lo", "core")
TEAM_AXES = ("y_hi", "x", "z")
ALL_AXES = BLK_AXES + TEAM_AXES
SIZES = {}


def fine_mesh(mesh):
    blk = mesh.shape["blk"]
    team = mesh.shape["team"]
    sizes = (blk // 2, 2, 2, 4, team // 8)
    SIZES.update(zip(ALL_AXES, sizes))
    return Mesh(mesh.devices.reshape(sizes), ALL_AXES)


def ring_offsets(n):
    offsets = [0]
    for step in range(1, n // 2 + 1):
        offsets.append(-step)
        if step < n - step:
            offsets.append(step)
    return offsets


class Chain:
    def __init__(self, value, steps):
        self.value = value
        self.steps = list(steps)

    def tick(self, values):
        if self.steps:
            self.value = self.steps.pop(0)(self.value)
        values, self.value = lax.optimization_barrier((values, self.value))
        return values

    def finish(self):
        while self.steps:
            self.value = self.steps.pop(0)(self.value)
        return self.value


def ring_gather(blocks, axis, chain=None):
    n = SIZES[axis]
    ahead = blocks
    behind = blocks
    parts = [blocks]
    for step in range(1, n // 2 + 1):
        ahead = lax.ppermute(ahead, axis, [(i, (i + 1) % n) for i in range(n)])
        if step < n - step:
            behind = lax.ppermute(behind, axis, [(i, (i - 1) % n) for i in range(n)])
        if chain is not None:
            ahead, behind = chain.tick((ahead, behind))
        parts.append(ahead)
        if step < n - step:
            parts.append(behind)
    return jnp.concatenate(parts, axis=0)


def gather_team(rows, chain=None):
    other = lax.ppermute(rows, "y_hi", perm=[(0, 1), (1, 0)])
    if chain is not None:
        other = chain.tick(other)
    pair = jnp.stack([rows, other], axis=0)
    full = ring_gather(ring_gather(pair, "x", chain), "z", chain)
    return full.reshape(-1, rows.shape[1])


def ring_slot(delta, axis):
    n = SIZES[axis]
    order = [o % n for o in ring_offsets(n)]
    table = [order.index(d) for d in range(n)]
    return jnp.asarray(table, jnp.int32)[(delta + n) % n]


def member_slots(members):
    nx, nz = SIZES["x"], SIZES["z"]
    m_hi = members // (nx * nz)
    m_x = (members // nz) % nx
    m_z = members % nz
    y_slot = (m_hi != lax.axis_index("y_hi")).astype(jnp.int32)
    x_slot = ring_slot(m_x - lax.axis_index("x"), "x")
    z_slot = ring_slot(m_z - lax.axis_index("z"), "z")
    return (z_slot * nx + x_slot) * 2 + y_slot


def swap(value, axis, bit):
    n = SIZES[axis]
    return lax.ppermute(value, axis, [(i, i ^ bit) for i in range(n)])


BUTTERFLY = (("y_lo", 1), ("x", 1), ("z", 1), ("y_lo", 2), ("x", 2), ("z", 2), ("z", 4), ("y_hi", 1))


def all_sum_steps():
    def split(value):
        half = value.shape[0] // 2
        upper = lax.axis_index("core") == 1
        keep = jnp.where(upper, value[half:], value[:half])
        send = jnp.where(upper, value[:half], value[half:])
        return keep + swap(send, "core", 1)

    def join(part):
        upper = lax.axis_index("core") == 1
        other = swap(part, "core", 1)
        return jnp.where(upper, jnp.concatenate([other, part]), jnp.concatenate([part, other]))

    steps = [split]
    for axis, bit in BUTTERFLY:
        if bit < SIZES[axis]:
            steps.append(lambda part, axis=axis, bit=bit: part + swap(part, axis, bit))
    steps.append(join)
    return steps


def blk_reduce_scatter(partial):
    width = partial.shape[-1]
    block = partial.shape[0] // (SIZES["y_lo"] * SIZES["core"])
    cur = partial.reshape(-1, 2, block, width)
    upper = lax.axis_index("core") == 1
    keep = jnp.where(upper, cur[:, 1], cur[:, 0])
    send = jnp.where(upper, cur[:, 0], cur[:, 1])
    cur = keep + swap(send, "core", 1)
    bit = 1
    while bit < SIZES["y_lo"]:
        cur = cur.reshape(-1, 2, block, width)
        upper = (lax.axis_index("y_lo") & bit) != 0
        keep = jnp.where(upper, cur[:, 1], cur[:, 0])
        send = jnp.where(upper, cur[:, 0], cur[:, 1])
        cur = keep + swap(send, "y_lo", bit)
        bit *= 2
    return cur.reshape(block, width)


def blk_all_gather_steps():
    steps = [lambda rows: rows[None]]
    bit = 1
    while bit < SIZES["y_lo"]:
        def double(cur, bit=bit):
            upper = (lax.axis_index("y_lo") & bit) != 0
            got = swap(cur, "y_lo", bit)
            return jnp.where(upper, jnp.concatenate([got, cur]), jnp.concatenate([cur, got]))
        steps.append(double)
        bit *= 2

    def cores(cur):
        upper = lax.axis_index("core") == 1
        got = swap(cur, "core", 1)
        both = jnp.where(upper, jnp.stack([got, cur], axis=1), jnp.stack([cur, got], axis=1))
        return both.reshape((-1,) + cur.shape[1:])

    steps.append(cores)
    return steps


def collect_kernel(slots_ref, vals_ref, panels_ref, out_ref):
    row = pl.program_id(0)
    nnz = vals_ref.shape[0]
    total = jnp.zeros(out_ref.shape, jnp.float32)
    for k in range(nnz):
        slot = slots_ref[row * nnz + k]
        total = total + jnp.dot(vals_ref[k], panels_ref[slot], preferred_element_type=jnp.float32)
    out_ref[...] = total


def collect(panels, slots, adj_vals):
    block = adj_vals.shape[-1]
    width = panels.shape[1]
    rows, nnz = slots.shape
    stacked = panels.reshape(panels.shape[0] // block, block, width)
    grid_spec = pltpu.PrefetchScalarGridSpec(
        num_scalar_prefetch=1,
        grid=(rows,),
        in_specs=[
            pl.BlockSpec((None, None, None, nnz, block, block), lambda r, s: (0, r, 0, 0, 0, 0)),
            pl.BlockSpec(stacked.shape, lambda r, s: (0, 0, 0)),
        ],
        out_specs=pl.BlockSpec((block, width), lambda r, s: (r, 0)),
    )
    return pl.pallas_call(
        collect_kernel,
        grid_spec=grid_spec,
        out_shape=jax.ShapeDtypeStruct((rows * block, width), jnp.float32),
        cost_estimate=pl.CostEstimate(
            flops=2 * rows * nnz * block * block * width,
            transcendentals=0,
            bytes_accessed=stacked.size * 2 + rows * nnz * block * block * 2 + rows * block * width * 4,
        ),
    )(slots.reshape(-1), adj_vals, stacked)


def activation(value):
    return jax.nn.gelu(value, approximate=True)


def local(features, weight, bias, cotangent, adj_cols, adj_vals):
    slots = member_slots(adj_cols[0, :, 0, :])
    width = features.shape[1]
    gathered = gather_team(features)
    partial_ax = collect(gathered, slots, adj_vals)
    partial_rows = jnp.dot(
        partial_ax,
        weight.astype(jnp.float32),
        precision=lax.Precision.HIGHEST,
        preferred_element_type=jnp.float32,
    )
    summed = blk_reduce_scatter(partial_rows)
    pre = summed + bias[None, :]
    activated, pullback = jax.vjp(activation, pre)
    hidden = activated.astype(jnp.bfloat16)
    pulled = pullback(cotangent.astype(jnp.float32))[0].astype(jnp.bfloat16)
    local_bias = jnp.sum(pulled.astype(jnp.float32), axis=0)

    def weight_partial(pulled_rows):
        local_weight = jnp.einsum(
            "rnf,rng->fg",
            partial_ax.reshape(pulled_rows.shape),
            pulled_rows.astype(jnp.float32),
            precision=lax.Precision.HIGHEST,
            preferred_element_type=jnp.float32,
        )
        filler = jnp.zeros((7, local_bias.shape[0]), jnp.float32)
        return jnp.concatenate([local_weight, local_bias[None, :], filler], axis=0)

    gather_steps = blk_all_gather_steps()
    sum_steps = all_sum_steps()
    steps = gather_steps[1:-1] + [lambda cur: sum_steps[0](weight_partial(gather_steps[-1](cur)))]
    chain = Chain(gather_steps[0](pulled), steps + sum_steps[1:])
    pulled_group = gather_team(pulled, chain)
    partial_back = collect(pulled_group, slots, adj_vals)
    spread = blk_reduce_scatter(partial_back).astype(jnp.bfloat16)
    both = chain.finish()
    grad_input = jnp.dot(spread, weight.T, preferred_element_type=jnp.float32).astype(jnp.bfloat16)
    return (hidden, grad_input, both[:width], both[width])


def solution(mesh):
    fine = fine_mesh(mesh)
    rows = P(ALL_AXES, None)
    return jax.shard_map(
        local,
        mesh=fine,
        in_specs=(
            rows,
            P(),
            P(),
            rows,
            P(TEAM_AXES, None, BLK_AXES, None),
            P(TEAM_AXES, None, BLK_AXES, None, None, None),
        ),
        out_specs=(rows, rows, P(), P()),
        check_vma=False,
    )
```

```python
import jax
import jax.numpy as jnp
from jax import lax
from jax.experimental import pallas as pl
from jax.experimental.pallas import tpu as pltpu
from jax.sharding import Mesh
from jax.sharding import PartitionSpec as P

BLK_AXES = ("y_lo", "core")
TEAM_AXES = ("y_hi", "x", "z")
ALL_AXES = BLK_AXES + TEAM_AXES
SIZES = {}


def fine_mesh(mesh):
    blk = mesh.shape["blk"]
    team = mesh.shape["team"]
    sizes = (blk // 2, 2, 2, 4, team // 8)
    SIZES.update(zip(ALL_AXES, sizes))
    return Mesh(mesh.devices.reshape(sizes), ALL_AXES)


def ring_offsets(n):
    offsets = [0]
    for step in range(1, n // 2 + 1):
        offsets.append(-step)
        if step < n - step:
            offsets.append(step)
    return offsets


def ring_gather(blocks, axis):
    n = SIZES[axis]
    ahead = blocks
    behind = blocks
    parts = [blocks]
    for step in range(1, n // 2 + 1):
        ahead = lax.ppermute(ahead, axis, [(i, (i + 1) % n) for i in range(n)])
        parts.append(ahead)
        if step < n - step:
            behind = lax.ppermute(behind, axis, [(i, (i - 1) % n) for i in range(n)])
            parts.append(behind)
    return jnp.concatenate(parts, axis=0)


def gather_team(rows):
    other = lax.ppermute(rows, "y_hi", perm=[(0, 1), (1, 0)])
    pair = jnp.stack([rows, other], axis=0)
    full = ring_gather(ring_gather(pair, "x"), "z")
    return full.reshape(-1, rows.shape[1])


def ring_slot(delta, axis):
    n = SIZES[axis]
    order = [o % n for o in ring_offsets(n)]
    table = [order.index(d) for d in range(n)]
    return jnp.asarray(table, jnp.int32)[(delta + n) % n]


def member_slots(members):
    nx, nz = SIZES["x"], SIZES["z"]
    m_hi = members // (nx * nz)
    m_x = (members // nz) % nx
    m_z = members % nz
    y_slot = (m_hi != lax.axis_index("y_hi")).astype(jnp.int32)
    x_slot = ring_slot(m_x - lax.axis_index("x"), "x")
    z_slot = ring_slot(m_z - lax.axis_index("z"), "z")
    return (z_slot * nx + x_slot) * 2 + y_slot


def swap(value, axis, bit):
    n = SIZES[axis]
    return lax.ppermute(value, axis, [(i, i ^ bit) for i in range(n)])


BUTTERFLY = (("y_lo", 1), ("x", 1), ("z", 1), ("y_lo", 2), ("x", 2), ("z", 2), ("z", 4), ("y_hi", 1))


def all_sum(value):
    half = value.shape[0] // 2
    upper = lax.axis_index("core") == 1
    low, high = value[:half], value[half:]
    keep = jnp.where(upper, high, low)
    send = jnp.where(upper, low, high)
    part = keep + swap(send, "core", 1)
    for axis, bit in BUTTERFLY:
        if bit < SIZES[axis]:
            part = part + swap(part, axis, bit)
    other = swap(part, "core", 1)
    return jnp.where(upper, jnp.concatenate([other, part]), jnp.concatenate([part, other]))


def blk_reduce_scatter(partial):
    width = partial.shape[-1]
    block = partial.shape[0] // (SIZES["y_lo"] * SIZES["core"])
    cur = partial.reshape(-1, 2, block, width)
    upper = lax.axis_index("core") == 1
    keep = jnp.where(upper, cur[:, 1], cur[:, 0])
    send = jnp.where(upper, cur[:, 0], cur[:, 1])
    cur = keep + swap(send, "core", 1)
    bit = 1
    while bit < SIZES["y_lo"]:
        cur = cur.reshape(-1, 2, block, width)
        upper = (lax.axis_index("y_lo") & bit) != 0
        keep = jnp.where(upper, cur[:, 1], cur[:, 0])
        send = jnp.where(upper, cur[:, 0], cur[:, 1])
        cur = keep + swap(send, "y_lo", bit)
        bit *= 2
    return cur.reshape(block, width)


def blk_all_gather(rows):
    cur = rows[None]
    bit = 1
    while bit < SIZES["y_lo"]:
        upper = (lax.axis_index("y_lo") & bit) != 0
        got = swap(cur, "y_lo", bit)
        cur = jnp.where(upper, jnp.concatenate([got, cur]), jnp.concatenate([cur, got]))
        bit *= 2
    upper = lax.axis_index("core") == 1
    got = swap(cur, "core", 1)
    cur = jnp.where(upper, jnp.stack([got, cur], axis=1), jnp.stack([cur, got], axis=1))
    return cur.reshape((-1,) + rows.shape)


def fused_collect_kernel(slots_ref, vals_ref, panels_ref, weight_ref, rows_ref, ax_ref, products):
    row = pl.program_id(0)
    nnz = vals_ref.shape[0]

    @pl.when(row == 0)
    def _():
        def one_panel(p, carry):
            products[p] = jnp.dot(
                panels_ref[p], weight_ref[...], preferred_element_type=jnp.float32
            ).astype(products.dtype)
            return carry

        lax.fori_loop(0, panels_ref.shape[0], one_panel, 0)

    total_rows = jnp.zeros(rows_ref.shape, jnp.float32)
    total_ax = jnp.zeros(ax_ref.shape, jnp.float32)
    for k in range(nnz):
        slot = slots_ref[row * nnz + k]
        values = vals_ref[k]
        total_rows = total_rows + jnp.dot(values, products[slot], preferred_element_type=jnp.float32)
        total_ax = total_ax + jnp.dot(values, panels_ref[slot], preferred_element_type=jnp.float32)
    rows_ref[...] = total_rows
    ax_ref[...] = total_ax


def fused_collect(panels, weight, slots, adj_vals):
    block = adj_vals.shape[-1]
    width = panels.shape[1]
    rows, nnz = slots.shape
    stacked = panels.reshape(panels.shape[0] // block, block, width)
    count = stacked.shape[0]
    grid_spec = pltpu.PrefetchScalarGridSpec(
        num_scalar_prefetch=1,
        grid=(rows,),
        in_specs=[
            pl.BlockSpec((None, None, None, nnz, block, block), lambda r, s: (0, r, 0, 0, 0, 0)),
            pl.BlockSpec(stacked.shape, lambda r, s: (0, 0, 0)),
            pl.BlockSpec(weight.shape, lambda r, s: (0, 0)),
        ],
        out_specs=[
            pl.BlockSpec((block, width), lambda r, s: (r, 0)),
            pl.BlockSpec((block, width), lambda r, s: (r, 0)),
        ],
        scratch_shapes=[pltpu.VMEM(stacked.shape, stacked.dtype)],
    )
    out = jax.ShapeDtypeStruct((rows * block, width), jnp.float32)
    return pl.pallas_call(
        fused_collect_kernel,
        grid_spec=grid_spec,
        out_shape=(out, out),
        compiler_params=pltpu.CompilerParams(dimension_semantics=("arbitrary",)),
        cost_estimate=pl.CostEstimate(
            flops=2 * count * block * width * width + 4 * rows * nnz * block * block * width,
            transcendentals=0,
            bytes_accessed=stacked.size * 2 + rows * nnz * block * block * 2 + 2 * rows * block * width * 4,
        ),
    )(slots.reshape(-1), adj_vals, stacked, weight)


def collect_kernel(slots_ref, vals_ref, panels_ref, out_ref):
    row = pl.program_id(0)
    nnz = vals_ref.shape[0]
    total = jnp.zeros(out_ref.shape, jnp.float32)
    for k in range(nnz):
        slot = slots_ref[row * nnz + k]
        total = total + jnp.dot(vals_ref[k], panels_ref[slot], preferred_element_type=jnp.float32)
    out_ref[...] = total


def collect(panels, slots, adj_vals):
    block = adj_vals.shape[-1]
    width = panels.shape[1]
    rows, nnz = slots.shape
    stacked = panels.reshape(panels.shape[0] // block, block, width)
    grid_spec = pltpu.PrefetchScalarGridSpec(
        num_scalar_prefetch=1,
        grid=(rows,),
        in_specs=[
            pl.BlockSpec((None, None, None, nnz, block, block), lambda r, s: (0, r, 0, 0, 0, 0)),
            pl.BlockSpec(stacked.shape, lambda r, s: (0, 0, 0)),
        ],
        out_specs=pl.BlockSpec((block, width), lambda r, s: (r, 0)),
    )
    return pl.pallas_call(
        collect_kernel,
        grid_spec=grid_spec,
        out_shape=jax.ShapeDtypeStruct((rows * block, width), jnp.float32),
        cost_estimate=pl.CostEstimate(
            flops=2 * rows * nnz * block * block * width,
            transcendentals=0,
            bytes_accessed=stacked.size * 2 + rows * nnz * block * block * 2 + rows * block * width * 4,
        ),
    )(slots.reshape(-1), adj_vals, stacked)


def activation(value):
    return jax.nn.gelu(value, approximate=True)


def local(features, weight, bias, cotangent, adj_cols, adj_vals):
    slots = member_slots(adj_cols[0, :, 0, :])
    width = features.shape[1]
    gathered = gather_team(features)
    partial_rows, partial_ax = fused_collect(gathered, weight, slots, adj_vals)
    summed = blk_reduce_scatter(partial_rows)
    pre = summed + bias[None, :]
    activated, pullback = jax.vjp(activation, pre)
    hidden = activated.astype(jnp.bfloat16)
    pulled = pullback(cotangent.astype(jnp.float32))[0].astype(jnp.bfloat16)
    pulled_rows = blk_all_gather(pulled)
    local_weight = jnp.einsum(
        "rnf,rng->fg",
        partial_ax.reshape(pulled_rows.shape),
        pulled_rows.astype(jnp.float32),
        precision=lax.Precision.HIGHEST,
        preferred_element_type=jnp.float32,
    )
    local_bias = jnp.sum(pulled.astype(jnp.float32), axis=0)
    filler = jnp.zeros((7, local_bias.shape[0]), jnp.float32)
    both = all_sum(jnp.concatenate([local_weight, local_bias[None, :], filler], axis=0))
    pulled_group = gather_team(pulled)
    partial_back = collect(pulled_group, slots, adj_vals)
    spread = blk_reduce_scatter(partial_back).astype(jnp.bfloat16)
    grad_input = jnp.dot(spread, weight.T, preferred_element_type=jnp.float32).astype(jnp.bfloat16)
    return (hidden, grad_input, both[:width], both[width])


def solution(mesh):
    fine = fine_mesh(mesh)
    rows = P(ALL_AXES, None)
    return jax.shard_map(
        local,
        mesh=fine,
        in_specs=(
            rows,
            P(),
            P(),
            rows,
            P(TEAM_AXES, None, BLK_AXES, None),
            P(TEAM_AXES, None, BLK_AXES, None, None, None),
        ),
        out_specs=(rows, rows, P(), P()),
        check_vma=False,
    )
```

```python
import jax
import jax.numpy as jnp
from jax import lax
from jax.experimental import pallas as pl
from jax.experimental.pallas import tpu as pltpu
from jax.sharding import Mesh
from jax.sharding import PartitionSpec as P

BLK_AXES = ("y_lo", "core")
TEAM_AXES = ("y_hi", "x", "z")
ALL_AXES = BLK_AXES + TEAM_AXES
SIZES = {}


def fine_mesh(mesh):
    blk = mesh.shape["blk"]
    team = mesh.shape["team"]
    sizes = (blk // 2, 2, 2, 4, team // 8)
    SIZES.update(zip(ALL_AXES, sizes))
    return Mesh(mesh.devices.reshape(sizes), ALL_AXES)


def ring_offsets(n):
    offsets = [0]
    for step in range(1, n // 2 + 1):
        offsets.append(-step)
        if step < n - step:
            offsets.append(step)
    return offsets


def ring_gather(blocks, axis):
    n = SIZES[axis]
    ahead = blocks
    behind = blocks
    parts = [blocks]
    for step in range(1, n // 2 + 1):
        ahead = lax.ppermute(ahead, axis, [(i, (i + 1) % n) for i in range(n)])
        parts.append(ahead)
        if step < n - step:
            behind = lax.ppermute(behind, axis, [(i, (i - 1) % n) for i in range(n)])
            parts.append(behind)
    return jnp.concatenate(parts, axis=0)


def gather_team(rows):
    other = lax.ppermute(rows, "y_hi", perm=[(0, 1), (1, 0)])
    pair = jnp.stack([rows, other], axis=0)
    full = ring_gather(ring_gather(pair, "x"), "z")
    return full.reshape(-1, rows.shape[1])


def ring_slot(delta, axis):
    n = SIZES[axis]
    order = [o % n for o in ring_offsets(n)]
    table = [order.index(d) for d in range(n)]
    return jnp.asarray(table, jnp.int32)[(delta + n) % n]


def member_slots(members):
    nx, nz = SIZES["x"], SIZES["z"]
    m_hi = members // (nx * nz)
    m_x = (members // nz) % nx
    m_z = members % nz
    y_slot = (m_hi != lax.axis_index("y_hi")).astype(jnp.int32)
    x_slot = ring_slot(m_x - lax.axis_index("x"), "x")
    z_slot = ring_slot(m_z - lax.axis_index("z"), "z")
    return (z_slot * nx + x_slot) * 2 + y_slot


def swap(value, axis, bit):
    n = SIZES[axis]
    return lax.ppermute(value, axis, [(i, i ^ bit) for i in range(n)])


BUTTERFLY = (("y_lo", 1), ("x", 1), ("z", 1), ("y_lo", 2), ("x", 2), ("z", 2), ("z", 4), ("y_hi", 1))


def all_sum(value):
    half = value.shape[0] // 2
    upper = lax.axis_index("core") == 1
    low, high = value[:half], value[half:]
    keep = jnp.where(upper, high, low)
    send = jnp.where(upper, low, high)
    part = keep + swap(send, "core", 1)
    for axis, bit in BUTTERFLY:
        if bit < SIZES[axis]:
            part = part + swap(part, axis, bit)
    other = swap(part, "core", 1)
    return jnp.where(upper, jnp.concatenate([other, part]), jnp.concatenate([part, other]))


def blk_reduce_scatter(partial):
    width = partial.shape[-1]
    block = partial.shape[0] // (SIZES["y_lo"] * SIZES["core"])
    cur = partial.reshape(-1, 2, block, width)
    upper = lax.axis_index("core") == 1
    keep = jnp.where(upper, cur[:, 1], cur[:, 0])
    send = jnp.where(upper, cur[:, 0], cur[:, 1])
    cur = keep + swap(send, "core", 1)
    bit = 1
    while bit < SIZES["y_lo"]:
        cur = cur.reshape(-1, 2, block, width)
        upper = (lax.axis_index("y_lo") & bit) != 0
        keep = jnp.where(upper, cur[:, 1], cur[:, 0])
        send = jnp.where(upper, cur[:, 0], cur[:, 1])
        cur = keep + swap(send, "y_lo", bit)
        bit *= 2
    return cur.reshape(block, width)


def blk_all_gather(rows):
    cur = rows[None]
    bit = 1
    while bit < SIZES["y_lo"]:
        upper = (lax.axis_index("y_lo") & bit) != 0
        got = swap(cur, "y_lo", bit)
        cur = jnp.where(upper, jnp.concatenate([got, cur]), jnp.concatenate([cur, got]))
        bit *= 2
    upper = lax.axis_index("core") == 1
    got = swap(cur, "core", 1)
    cur = jnp.where(upper, jnp.stack([got, cur], axis=1), jnp.stack([cur, got], axis=1))
    return cur.reshape((-1,) + rows.shape)


def collect_kernel(slots_ref, vals_ref, panels_hbm, out_ref, held, sems):
    row = pl.program_id(0)
    rows = pl.num_programs(0)
    nnz = vals_ref.shape[0]

    def fetch(target, buffer):
        for k in range(nnz):
            pltpu.make_async_copy(
                panels_hbm.at[slots_ref[target * nnz + k]], held.at[buffer, k], sems.at[buffer, k]
            ).start()

    @pl.when(row == 0)
    def _():
        fetch(0, 0)

    @pl.when(row + 1 < rows)
    def _():
        fetch(row + 1, (row + 1) % 2)

    current = row % 2
    total = jnp.zeros(out_ref.shape, jnp.float32)
    for k in range(nnz):
        pltpu.make_async_copy(panels_hbm.at[0], held.at[current, k], sems.at[current, k]).wait()
        total = total + jnp.dot(vals_ref[k], held[current, k], preferred_element_type=jnp.float32)
    out_ref[...] = total


def collect(panels, slots, adj_vals):
    block = adj_vals.shape[-1]
    width = panels.shape[1]
    rows, nnz = slots.shape
    stacked = panels.reshape(panels.shape[0] // block, block, width)
    grid_spec = pltpu.PrefetchScalarGridSpec(
        num_scalar_prefetch=1,
        grid=(rows,),
        in_specs=[
            pl.BlockSpec((None, None, None, nnz, block, block), lambda r, s: (0, r, 0, 0, 0, 0)),
            pl.BlockSpec(memory_space=pl.ANY),
        ],
        out_specs=pl.BlockSpec((block, width), lambda r, s: (r, 0)),
        scratch_shapes=[
            pltpu.VMEM((2, nnz, block, width), stacked.dtype),
            pltpu.SemaphoreType.DMA((2, nnz)),
        ],
    )
    return pl.pallas_call(
        collect_kernel,
        grid_spec=grid_spec,
        out_shape=jax.ShapeDtypeStruct((rows * block, width), jnp.float32),
        compiler_params=pltpu.CompilerParams(dimension_semantics=("arbitrary",)),
        cost_estimate=pl.CostEstimate(
            flops=2 * rows * nnz * block * block * width,
            transcendentals=0,
            bytes_accessed=rows * nnz * block * (block + width) * 2 + rows * block * width * 4,
        ),
    )(slots.reshape(-1), adj_vals, stacked)


def activation(value):
    return jax.nn.gelu(value, approximate=True)


def local(features, weight, bias, cotangent, adj_cols, adj_vals):
    slots = member_slots(adj_cols[0, :, 0, :])
    width = features.shape[1]
    gathered = gather_team(features)
    products = jnp.dot(gathered, weight, preferred_element_type=jnp.float32).astype(jnp.bfloat16)
    partial_rows = collect(products, slots, adj_vals)
    partial_ax = collect(gathered, slots, adj_vals)
    summed = blk_reduce_scatter(partial_rows)
    pre = summed + bias[None, :]
    activated, pullback = jax.vjp(activation, pre)
    hidden = activated.astype(jnp.bfloat16)
    pulled = pullback(cotangent.astype(jnp.float32))[0].astype(jnp.bfloat16)
    pulled_rows = blk_all_gather(pulled)
    local_weight = jnp.einsum(
        "rnf,rng->fg",
        partial_ax.reshape(pulled_rows.shape),
        pulled_rows.astype(jnp.float32),
        precision=lax.Precision.HIGHEST,
        preferred_element_type=jnp.float32,
    )
    local_bias = jnp.sum(pulled.astype(jnp.float32), axis=0)
    filler = jnp.zeros((7, local_bias.shape[0]), jnp.float32)
    both = all_sum(jnp.concatenate([local_weight, local_bias[None, :], filler], axis=0))
    pulled_group = gather_team(pulled)
    partial_back = collect(pulled_group, slots, adj_vals)
    spread = blk_reduce_scatter(partial_back).astype(jnp.bfloat16)
    grad_input = jnp.dot(spread, weight.T, preferred_element_type=jnp.float32).astype(jnp.bfloat16)
    return (hidden, grad_input, both[:width], both[width])


def solution(mesh):
    fine = fine_mesh(mesh)
    rows = P(ALL_AXES, None)
    return jax.shard_map(
        local,
        mesh=fine,
        in_specs=(
            rows,
            P(),
            P(),
            rows,
            P(TEAM_AXES, None, BLK_AXES, None),
            P(TEAM_AXES, None, BLK_AXES, None, None, None),
        ),
        out_specs=(rows, rows, P(), P()),
        check_vma=False,
    )
```

```python
import jax
import jax.numpy as jnp
from jax import lax
from jax.experimental import pallas as pl
from jax.experimental.pallas import tpu as pltpu
from jax.sharding import Mesh
from jax.sharding import PartitionSpec as P

BLK_AXES = ("y_lo", "core")
TEAM_AXES = ("y_hi", "x", "z")
ALL_AXES = BLK_AXES + TEAM_AXES
SIZES = {}


def fine_mesh(mesh):
    blk = mesh.shape["blk"]
    team = mesh.shape["team"]
    sizes = (blk // 2, 2, 2, 4, team // 8)
    SIZES.update(zip(ALL_AXES, sizes))
    return Mesh(mesh.devices.reshape(sizes), ALL_AXES)


def ring_offsets(n):
    offsets = [0]
    for step in range(1, n // 2 + 1):
        offsets.append(-step)
        if step < n - step:
            offsets.append(step)
    return offsets


class Chain:
    def __init__(self, value, steps):
        self.value = value
        self.steps = list(steps)

    def tick(self, values, count=1):
        for _ in range(count):
            if self.steps:
                self.value = self.steps.pop(0)(self.value)
        values, self.value = lax.optimization_barrier((values, self.value))
        return values

    def finish(self):
        while self.steps:
            self.value = self.steps.pop(0)(self.value)
        return self.value


def ring_gather(blocks, axis, chain=None, per_round=1):
    n = SIZES[axis]
    ahead = blocks
    behind = blocks
    parts = [blocks]
    for step in range(1, n // 2 + 1):
        ahead = lax.ppermute(ahead, axis, [(i, (i + 1) % n) for i in range(n)])
        if step < n - step:
            behind = lax.ppermute(behind, axis, [(i, (i - 1) % n) for i in range(n)])
        if chain is not None:
            ahead, behind = chain.tick((ahead, behind), per_round)
        parts.append(ahead)
        if step < n - step:
            parts.append(behind)
    return jnp.concatenate(parts, axis=0)


def gather_team(rows, chain=None):
    other = lax.ppermute(rows, "y_hi", perm=[(0, 1), (1, 0)])
    if chain is not None:
        other = chain.tick(other)
    pair = jnp.stack([rows, other], axis=0)
    full = ring_gather(ring_gather(pair, "x", chain), "z", chain, 2)
    return full.reshape(-1, rows.shape[1])


def ring_slot(delta, axis):
    n = SIZES[axis]
    order = [o % n for o in ring_offsets(n)]
    table = [order.index(d) for d in range(n)]
    return jnp.asarray(table, jnp.int32)[(delta + n) % n]


def member_slots(members):
    nx, nz = SIZES["x"], SIZES["z"]
    m_hi = members // (nx * nz)
    m_x = (members // nz) % nx
    m_z = members % nz
    y_slot = (m_hi != lax.axis_index("y_hi")).astype(jnp.int32)
    x_slot = ring_slot(m_x - lax.axis_index("x"), "x")
    z_slot = ring_slot(m_z - lax.axis_index("z"), "z")
    return (z_slot * nx + x_slot) * 2 + y_slot


def swap(value, axis, bit):
    n = SIZES[axis]
    return lax.ppermute(value, axis, [(i, i ^ bit) for i in range(n)])


BUTTERFLY = (("y_lo", 1), ("x", 1), ("z", 1), ("y_lo", 2), ("x", 2), ("z", 2), ("z", 4), ("y_hi", 1))


def all_sum_steps():
    def split(value):
        half = value.shape[0] // 2
        upper = lax.axis_index("core") == 1
        keep = jnp.where(upper, value[half:], value[:half])
        send = jnp.where(upper, value[:half], value[half:])
        return keep + swap(send, "core", 1)

    def join(part):
        upper = lax.axis_index("core") == 1
        other = swap(part, "core", 1)
        return jnp.where(upper, jnp.concatenate([other, part]), jnp.concatenate([part, other]))

    steps = [split]
    for axis, bit in BUTTERFLY:
        if bit < SIZES[axis]:
            steps.append(lambda part, axis=axis, bit=bit: part + swap(part, axis, bit))
    steps.append(join)
    return steps


def blk_reduce_scatter(partial):
    width = partial.shape[-1]
    block = partial.shape[0] // (SIZES["y_lo"] * SIZES["core"])
    cur = partial.reshape(-1, 2, block, width)
    upper = lax.axis_index("core") == 1
    keep = jnp.where(upper, cur[:, 1], cur[:, 0])
    send = jnp.where(upper, cur[:, 0], cur[:, 1])
    cur = keep + swap(send, "core", 1)
    bit = 1
    while bit < SIZES["y_lo"]:
        cur = cur.reshape(-1, 2, block, width)
        upper = (lax.axis_index("y_lo") & bit) != 0
        keep = jnp.where(upper, cur[:, 1], cur[:, 0])
        send = jnp.where(upper, cur[:, 0], cur[:, 1])
        cur = keep + swap(send, "y_lo", bit)
        bit *= 2
    return cur.reshape(block, width)


def blk_all_gather_steps():
    steps = [lambda rows: rows[None]]
    bit = 1
    while bit < SIZES["y_lo"]:
        def double(cur, bit=bit):
            upper = (lax.axis_index("y_lo") & bit) != 0
            got = swap(cur, "y_lo", bit)
            return jnp.where(upper, jnp.concatenate([got, cur]), jnp.concatenate([cur, got]))
        steps.append(double)
        bit *= 2

    def cores(cur):
        upper = lax.axis_index("core") == 1
        got = swap(cur, "core", 1)
        both = jnp.where(upper, jnp.stack([got, cur], axis=1), jnp.stack([cur, got], axis=1))
        return both.reshape((-1,) + cur.shape[1:])

    steps.append(cores)
    return steps


def collect_kernel(slots_ref, vals_ref, panels_ref, out_ref):
    row = pl.program_id(0)
    nnz = vals_ref.shape[0]
    total = jnp.zeros(out_ref.shape, jnp.float32)
    for k in range(nnz):
        slot = slots_ref[row * nnz + k]
        total = total + jnp.dot(vals_ref[k], panels_ref[slot], preferred_element_type=jnp.float32)
    out_ref[...] = total


def collect(panels, slots, adj_vals):
    block = adj_vals.shape[-1]
    width = panels.shape[1]
    rows, nnz = slots.shape
    stacked = panels.reshape(panels.shape[0] // block, block, width)
    grid_spec = pltpu.PrefetchScalarGridSpec(
        num_scalar_prefetch=1,
        grid=(rows,),
        in_specs=[
            pl.BlockSpec((None, None, None, nnz, block, block), lambda r, s: (0, r, 0, 0, 0, 0)),
            pl.BlockSpec(stacked.shape, lambda r, s: (0, 0, 0)),
        ],
        out_specs=pl.BlockSpec((block, width), lambda r, s: (r, 0)),
    )
    return pl.pallas_call(
        collect_kernel,
        grid_spec=grid_spec,
        out_shape=jax.ShapeDtypeStruct((rows * block, width), jnp.float32),
        cost_estimate=pl.CostEstimate(
            flops=2 * rows * nnz * block * block * width,
            transcendentals=0,
            bytes_accessed=stacked.size * 2 + rows * nnz * block * block * 2 + rows * block * width * 4,
        ),
    )(slots.reshape(-1), adj_vals, stacked)


def activation(value):
    return jax.nn.gelu(value, approximate=True)


def local(features, weight, bias, cotangent, adj_cols, adj_vals):
    slots = member_slots(adj_cols[0, :, 0, :])
    width = features.shape[1]
    gathered = gather_team(features)
    partial_ax = collect(gathered, slots, adj_vals)
    partial_rows = jnp.dot(
        partial_ax,
        weight.astype(jnp.float32),
        precision=lax.Precision.HIGHEST,
        preferred_element_type=jnp.float32,
    )
    summed = blk_reduce_scatter(partial_rows)
    pre = summed + bias[None, :]
    activated, pullback = jax.vjp(activation, pre)
    hidden = activated.astype(jnp.bfloat16)
    pulled = pullback(cotangent.astype(jnp.float32))[0].astype(jnp.bfloat16)
    local_bias = jnp.sum(pulled.astype(jnp.float32), axis=0)

    def weight_partial(pulled_rows):
        local_weight = jnp.einsum(
            "rnf,rng->fg",
            partial_ax.reshape(pulled_rows.shape),
            pulled_rows.astype(jnp.float32),
            precision=lax.Precision.HIGHEST,
            preferred_element_type=jnp.float32,
        )
        filler = jnp.zeros((7, local_bias.shape[0]), jnp.float32)
        return jnp.concatenate([local_weight, local_bias[None, :], filler], axis=0)

    gather_steps = blk_all_gather_steps()
    sum_steps = all_sum_steps()
    steps = gather_steps[1:-1] + [lambda cur: sum_steps[0](weight_partial(gather_steps[-1](cur)))]
    chain = Chain(gather_steps[0](pulled), steps + sum_steps[1:])
    pulled_group = gather_team(pulled, chain)
    partial_back = collect(pulled_group, slots, adj_vals)
    spread = blk_reduce_scatter(partial_back).astype(jnp.bfloat16)
    both = chain.finish()
    grad_input = jnp.dot(spread, weight.T, preferred_element_type=jnp.float32).astype(jnp.bfloat16)
    return (hidden, grad_input, both[:width], both[width])


def solution(mesh):
    fine = fine_mesh(mesh)
    rows = P(ALL_AXES, None)
    return jax.shard_map(
        local,
        mesh=fine,
        in_specs=(
            rows,
            P(),
            P(),
            rows,
            P(TEAM_AXES, None, BLK_AXES, None),
            P(TEAM_AXES, None, BLK_AXES, None, None, None),
        ),
        out_specs=(rows, rows, P(), P()),
        check_vma=False,
    )
```

```python
import functools

import jax
import jax.numpy as jnp
from jax import lax
from jax.experimental import pallas as pl
from jax.experimental.pallas import tpu as pltpu
from jax.sharding import Mesh
from jax.sharding import PartitionSpec as P

BLK_AXES = ("y_lo", "core")
TEAM_AXES = ("y_hi", "x", "z")
ALL_AXES = BLK_AXES + TEAM_AXES
SIZES = {}


def fine_mesh(mesh):
    blk = mesh.shape["blk"]
    team = mesh.shape["team"]
    sizes = (blk // 2, 2, 2, 4, team // 8)
    SIZES.update(zip(ALL_AXES, sizes))
    return Mesh(mesh.devices.reshape(sizes), ALL_AXES)


def ring_offsets(n):
    offsets = [0]
    for step in range(1, n // 2 + 1):
        offsets.append(-step)
        if step < n - step:
            offsets.append(step)
    return offsets


class Chain:
    def __init__(self, value, steps):
        self.value = value
        self.steps = list(steps)

    def tick(self, values, count=1):
        for _ in range(count):
            if self.steps:
                self.value = self.steps.pop(0)(self.value)
        values, self.value = lax.optimization_barrier((values, self.value))
        return values

    def finish(self):
        while self.steps:
            self.value = self.steps.pop(0)(self.value)
        return self.value


def ring_gather(blocks, axis, chain=None, per_round=1, join=True):
    n = SIZES[axis]
    ahead = blocks
    behind = blocks
    parts = [blocks]
    for step in range(1, n // 2 + 1):
        ahead = lax.ppermute(ahead, axis, [(i, (i + 1) % n) for i in range(n)])
        if step < n - step:
            behind = lax.ppermute(behind, axis, [(i, (i - 1) % n) for i in range(n)])
        if chain is not None:
            ahead, behind = chain.tick((ahead, behind), per_round)
        parts.append(ahead)
        if step < n - step:
            parts.append(behind)
    return jnp.concatenate(parts, axis=0) if join else parts


def gather_team(rows, chain=None):
    other = lax.ppermute(rows, "y_hi", perm=[(0, 1), (1, 0)])
    if chain is not None:
        other = chain.tick(other)
    pair = jnp.stack([rows, other], axis=0)
    return ring_gather(ring_gather(pair, "x", chain), "z", chain, 2, join=False)


def ring_slot(delta, axis):
    n = SIZES[axis]
    order = [o % n for o in ring_offsets(n)]
    table = [order.index(d) for d in range(n)]
    return jnp.asarray(table, jnp.int32)[(delta + n) % n]


def member_slots(members):
    nx, nz = SIZES["x"], SIZES["z"]
    m_hi = members // (nx * nz)
    m_x = (members // nz) % nx
    m_z = members % nz
    y_slot = (m_hi != lax.axis_index("y_hi")).astype(jnp.int32)
    x_slot = ring_slot(m_x - lax.axis_index("x"), "x")
    z_slot = ring_slot(m_z - lax.axis_index("z"), "z")
    return (z_slot * nx + x_slot) * 2 + y_slot


def swap(value, axis, bit):
    n = SIZES[axis]
    return lax.ppermute(value, axis, [(i, i ^ bit) for i in range(n)])


BUTTERFLY = (("y_lo", 1), ("x", 1), ("z", 1), ("y_lo", 2), ("x", 2), ("z", 2), ("z", 4), ("y_hi", 1))


def all_sum_steps():
    def split(value):
        half = value.shape[0] // 2
        upper = lax.axis_index("core") == 1
        keep = jnp.where(upper, value[half:], value[:half])
        send = jnp.where(upper, value[:half], value[half:])
        return keep + swap(send, "core", 1)

    def join(part):
        upper = lax.axis_index("core") == 1
        other = swap(part, "core", 1)
        return jnp.where(upper, jnp.concatenate([other, part]), jnp.concatenate([part, other]))

    steps = [split]
    for axis, bit in BUTTERFLY:
        if bit < SIZES[axis]:
            steps.append(lambda part, axis=axis, bit=bit: part + swap(part, axis, bit))
    steps.append(join)
    return steps


def blk_reduce_scatter(partial):
    width = partial.shape[-1]
    block = partial.shape[0] // (SIZES["y_lo"] * SIZES["core"])
    cur = partial.reshape(-1, 2, block, width)
    upper = lax.axis_index("core") == 1
    keep = jnp.where(upper, cur[:, 1], cur[:, 0])
    send = jnp.where(upper, cur[:, 0], cur[:, 1])
    cur = keep + swap(send, "core", 1)
    bit = 1
    while bit < SIZES["y_lo"]:
        cur = cur.reshape(-1, 2, block, width)
        upper = (lax.axis_index("y_lo") & bit) != 0
        keep = jnp.where(upper, cur[:, 1], cur[:, 0])
        send = jnp.where(upper, cur[:, 0], cur[:, 1])
        cur = keep + swap(send, "y_lo", bit)
        bit *= 2
    return cur.reshape(block, width)


def blk_all_gather_steps():
    steps = [lambda rows: rows[None]]
    bit = 1
    while bit < SIZES["y_lo"]:
        def double(cur, bit=bit):
            upper = (lax.axis_index("y_lo") & bit) != 0
            got = swap(cur, "y_lo", bit)
            return jnp.where(upper, jnp.concatenate([got, cur]), jnp.concatenate([cur, got]))
        steps.append(double)
        bit *= 2

    def cores(cur):
        upper = lax.axis_index("core") == 1
        got = swap(cur, "core", 1)
        both = jnp.where(upper, jnp.stack([got, cur], axis=1), jnp.stack([cur, got], axis=1))
        return both.reshape((-1,) + cur.shape[1:])

    steps.append(cores)
    return steps


def collect_kernel(count, slots_ref, vals_ref, *refs):
    parts = refs[:count]
    out_ref, held, sems = refs[count:]
    row = pl.program_id(0)
    nnz = vals_ref.shape[0]
    size = held.shape[0] // count

    @pl.when(row == 0)
    def _():
        copies = [
            pltpu.make_async_copy(parts[i], held.at[pl.ds(i * size, size)], sems.at[i])
            for i in range(count)
        ]
        for copy in copies:
            copy.start()
        for copy in copies:
            copy.wait()

    total = jnp.zeros(out_ref.shape, jnp.float32)
    for k in range(nnz):
        slot = slots_ref[row * nnz + k]
        total = total + jnp.dot(vals_ref[k], held[slot], preferred_element_type=jnp.float32)
    out_ref[...] = total


def collect(parts, slots, adj_vals):
    block = adj_vals.shape[-1]
    width = parts[0].shape[-1]
    rows, nnz = slots.shape
    count = len(parts)
    panels = count * parts[0].shape[0]
    grid_spec = pltpu.PrefetchScalarGridSpec(
        num_scalar_prefetch=1,
        grid=(rows,),
        in_specs=[pl.BlockSpec((None, None, None, nnz, block, block), lambda r, s: (0, r, 0, 0, 0, 0))]
        + [pl.BlockSpec(memory_space=pl.ANY)] * count,
        out_specs=pl.BlockSpec((block, width), lambda r, s: (r, 0)),
        scratch_shapes=[
            pltpu.VMEM((panels, block, width), parts[0].dtype),
            pltpu.SemaphoreType.DMA((count,)),
        ],
    )
    return pl.pallas_call(
        functools.partial(collect_kernel, count),
        grid_spec=grid_spec,
        out_shape=jax.ShapeDtypeStruct((rows * block, width), jnp.float32),
        compiler_params=pltpu.CompilerParams(dimension_semantics=("arbitrary",)),
        cost_estimate=pl.CostEstimate(
            flops=2 * rows * nnz * block * block * width,
            transcendentals=0,
            bytes_accessed=panels * block * width * 2 + rows * nnz * block * block * 2 + rows * block * width * 4,
        ),
    )(slots.reshape(-1), adj_vals, *parts)


def activation(value):
    return jax.nn.gelu(value, approximate=True)


def local(features, weight, bias, cotangent, adj_cols, adj_vals):
    slots = member_slots(adj_cols[0, :, 0, :])
    width = features.shape[1]
    gathered = gather_team(features)
    partial_ax = collect(gathered, slots, adj_vals)
    partial_rows = jnp.dot(
        partial_ax,
        weight.astype(jnp.float32),
        precision=lax.Precision.HIGHEST,
        preferred_element_type=jnp.float32,
    )
    summed = blk_reduce_scatter(partial_rows)
    pre = summed + bias[None, :]
    activated, pullback = jax.vjp(activation, pre)
    hidden = activated.astype(jnp.bfloat16)
    pulled = pullback(cotangent.astype(jnp.float32))[0].astype(jnp.bfloat16)
    local_bias = jnp.sum(pulled.astype(jnp.float32), axis=0)

    def weight_partial(pulled_rows):
        local_weight = jnp.einsum(
            "rnf,rng->fg",
            partial_ax.reshape(pulled_rows.shape),
            pulled_rows.astype(jnp.float32),
            precision=lax.Precision.HIGHEST,
            preferred_element_type=jnp.float32,
        )
        filler = jnp.zeros((7, local_bias.shape[0]), jnp.float32)
        return jnp.concatenate([local_weight, local_bias[None, :], filler], axis=0)

    gather_steps = blk_all_gather_steps()
    sum_steps = all_sum_steps()
    steps = gather_steps[1:-1] + [lambda cur: sum_steps[0](weight_partial(gather_steps[-1](cur)))]
    chain = Chain(gather_steps[0](pulled), steps + sum_steps[1:])
    pulled_group = gather_team(pulled, chain)
    partial_back = collect(pulled_group, slots, adj_vals)
    spread = blk_reduce_scatter(partial_back).astype(jnp.bfloat16)
    both = chain.finish()
    grad_input = jnp.dot(spread, weight.T, preferred_element_type=jnp.float32).astype(jnp.bfloat16)
    return (hidden, grad_input, both[:width], both[width])


def solution(mesh):
    fine = fine_mesh(mesh)
    rows = P(ALL_AXES, None)
    return jax.shard_map(
        local,
        mesh=fine,
        in_specs=(
            rows,
            P(),
            P(),
            rows,
            P(TEAM_AXES, None, BLK_AXES, None),
            P(TEAM_AXES, None, BLK_AXES, None, None, None),
        ),
        out_specs=(rows, rows, P(), P()),
        check_vma=False,
    )
```

```python
import functools

import jax
import jax.numpy as jnp
from jax import lax
from jax.experimental import pallas as pl
from jax.experimental.pallas import tpu as pltpu
from jax.sharding import Mesh
from jax.sharding import PartitionSpec as P

BLK_AXES = ("y_lo", "core")
TEAM_AXES = ("y_hi", "x", "z")
ALL_AXES = BLK_AXES + TEAM_AXES
SIZES = {}


def fine_mesh(mesh):
    blk = mesh.shape["blk"]
    team = mesh.shape["team"]
    sizes = (blk // 2, 2, 2, 4, team // 8)
    SIZES.update(zip(ALL_AXES, sizes))
    return Mesh(mesh.devices.reshape(sizes), ALL_AXES)


def ring_offsets(n):
    offsets = [0]
    for step in range(1, n // 2 + 1):
        offsets.append(-step)
        if step < n - step:
            offsets.append(step)
    return offsets


class Chain:
    def __init__(self, value, steps):
        self.value = value
        self.steps = list(steps)

    def tick(self, values, count=1):
        for _ in range(count):
            if self.steps:
                self.value = self.steps.pop(0)(self.value)
        values, self.value = lax.optimization_barrier((values, self.value))
        return values

    def finish(self):
        while self.steps:
            self.value = self.steps.pop(0)(self.value)
        return self.value


def ring_gather(blocks, axis, chain=None, per_round=1, join=True):
    n = SIZES[axis]
    ahead = blocks
    behind = blocks
    parts = [blocks]
    for step in range(1, n // 2 + 1):
        ahead = lax.ppermute(ahead, axis, [(i, (i + 1) % n) for i in range(n)])
        if step < n - step:
            behind = lax.ppermute(behind, axis, [(i, (i - 1) % n) for i in range(n)])
        if chain is not None:
            ahead, behind = chain.tick((ahead, behind), per_round)
        parts.append(ahead)
        if step < n - step:
            parts.append(behind)
    return jnp.concatenate(parts, axis=0) if join else parts


def gather_team(rows, chain=None):
    other = lax.ppermute(rows, "y_hi", perm=[(0, 1), (1, 0)])
    if chain is not None:
        other = chain.tick(other)
    pair = jnp.stack([rows, other], axis=0)
    return ring_gather(ring_gather(pair, "x", chain), "z", chain, 2, join=False)


def ring_slot(delta, axis):
    n = SIZES[axis]
    order = [o % n for o in ring_offsets(n)]
    table = [order.index(d) for d in range(n)]
    return jnp.asarray(table, jnp.int32)[(delta + n) % n]


def member_slots(members):
    nx, nz = SIZES["x"], SIZES["z"]
    m_hi = members // (nx * nz)
    m_x = (members // nz) % nx
    m_z = members % nz
    y_slot = (m_hi != lax.axis_index("y_hi")).astype(jnp.int32)
    x_slot = ring_slot(m_x - lax.axis_index("x"), "x")
    z_slot = ring_slot(m_z - lax.axis_index("z"), "z")
    return (z_slot * nx + x_slot) * 2 + y_slot


def swap(value, axis, bit):
    n = SIZES[axis]
    return lax.ppermute(value, axis, [(i, i ^ bit) for i in range(n)])


BUTTERFLY = (("y_lo", 1), ("x", 1), ("z", 1), ("y_lo", 2), ("x", 2), ("z", 2), ("z", 4), ("y_hi", 1))


def all_sum_steps():
    def split(value):
        half = value.shape[0] // 2
        upper = lax.axis_index("core") == 1
        keep = jnp.where(upper, value[half:], value[:half])
        send = jnp.where(upper, value[:half], value[half:])
        return keep + swap(send, "core", 1)

    def join(part):
        upper = lax.axis_index("core") == 1
        other = swap(part, "core", 1)
        return jnp.where(upper, jnp.concatenate([other, part]), jnp.concatenate([part, other]))

    steps = [split]
    for axis, bit in BUTTERFLY:
        if bit < SIZES[axis]:
            steps.append(lambda part, axis=axis, bit=bit: part + swap(part, axis, bit))
    steps.append(join)
    return steps


def blk_reduce_scatter(partial):
    width = partial.shape[-1]
    block = partial.shape[0] // (SIZES["y_lo"] * SIZES["core"])
    cur = partial.reshape(-1, 2, block, width)
    upper = lax.axis_index("core") == 1
    keep = jnp.where(upper, cur[:, 1], cur[:, 0])
    send = jnp.where(upper, cur[:, 0], cur[:, 1])
    cur = keep + swap(send, "core", 1)
    bit = 1
    while bit < SIZES["y_lo"]:
        cur = cur.reshape(-1, 2, block, width)
        upper = (lax.axis_index("y_lo") & bit) != 0
        keep = jnp.where(upper, cur[:, 1], cur[:, 0])
        send = jnp.where(upper, cur[:, 0], cur[:, 1])
        cur = keep + swap(send, "y_lo", bit)
        bit *= 2
    return cur.reshape(block, width)


def blk_all_gather_steps():
    steps = [lambda rows: rows[None]]
    bit = 1
    while bit < SIZES["y_lo"]:
        def double(cur, bit=bit):
            upper = (lax.axis_index("y_lo") & bit) != 0
            got = swap(cur, "y_lo", bit)
            return jnp.where(upper, jnp.concatenate([got, cur]), jnp.concatenate([cur, got]))
        steps.append(double)
        bit *= 2

    def cores(cur):
        upper = lax.axis_index("core") == 1
        got = swap(cur, "core", 1)
        both = jnp.where(upper, jnp.stack([got, cur], axis=1), jnp.stack([cur, got], axis=1))
        return both.reshape((-1,) + cur.shape[1:])

    steps.append(cores)
    return steps


def collect_kernel(count, with_weight, slots_ref, vals_ref, *refs):
    parts = refs[:count]
    if with_weight:
        weight_ref, out_ref, mixed_ref, held, sems = refs[count:]
    else:
        out_ref, held, sems = refs[count:]
    row = pl.program_id(0)
    nnz = vals_ref.shape[0]
    size = held.shape[0] // count

    @pl.when(row == 0)
    def _():
        copies = [
            pltpu.make_async_copy(parts[i], held.at[pl.ds(i * size, size)], sems.at[i])
            for i in range(count)
        ]
        for copy in copies:
            copy.start()
        for copy in copies:
            copy.wait()

    total = jnp.zeros(out_ref.shape, jnp.float32)
    for k in range(nnz):
        slot = slots_ref[row * nnz + k]
        total = total + jnp.dot(vals_ref[k], held[slot], preferred_element_type=jnp.float32)
    out_ref[...] = total
    if with_weight:
        mixed_ref[...] = jnp.dot(
            total,
            weight_ref[...].astype(jnp.float32),
            precision=lax.Precision.HIGHEST,
            preferred_element_type=jnp.float32,
        )


def collect(parts, slots, adj_vals, weight=None):
    block = adj_vals.shape[-1]
    width = parts[0].shape[-1]
    rows, nnz = slots.shape
    count = len(parts)
    panels = count * parts[0].shape[0]
    with_weight = weight is not None
    row_spec = pl.BlockSpec((block, width), lambda r, s: (r, 0))
    out = jax.ShapeDtypeStruct((rows * block, width), jnp.float32)
    extra = [pl.BlockSpec(weight.shape, lambda r, s: (0, 0))] if with_weight else []
    grid_spec = pltpu.PrefetchScalarGridSpec(
        num_scalar_prefetch=1,
        grid=(rows,),
        in_specs=[pl.BlockSpec((None, None, None, nnz, block, block), lambda r, s: (0, r, 0, 0, 0, 0))]
        + [pl.BlockSpec(memory_space=pl.ANY)] * count
        + extra,
        out_specs=[row_spec, row_spec] if with_weight else row_spec,
        scratch_shapes=[
            pltpu.VMEM((panels, block, width), parts[0].dtype),
            pltpu.SemaphoreType.DMA((count,)),
        ],
    )
    operands = [slots.reshape(-1), adj_vals, *parts] + ([weight] if with_weight else [])
    return pl.pallas_call(
        functools.partial(collect_kernel, count, with_weight),
        grid_spec=grid_spec,
        out_shape=(out, out) if with_weight else out,
        compiler_params=pltpu.CompilerParams(dimension_semantics=("arbitrary",)),
        cost_estimate=pl.CostEstimate(
            flops=2 * rows * nnz * block * block * width + (6 * rows * block * width * width if with_weight else 0),
            transcendentals=0,
            bytes_accessed=panels * block * width * 2 + rows * nnz * block * block * 2 + rows * block * width * 4,
        ),
    )(*operands)


def activation(value):
    return jax.nn.gelu(value, approximate=True)


def local(features, weight, bias, cotangent, adj_cols, adj_vals):
    slots = member_slots(adj_cols[0, :, 0, :])
    width = features.shape[1]
    gathered = gather_team(features)
    partial_ax, partial_rows = collect(gathered, slots, adj_vals, weight)
    summed = blk_reduce_scatter(partial_rows)
    pre = summed + bias[None, :]
    activated, pullback = jax.vjp(activation, pre)
    hidden = activated.astype(jnp.bfloat16)
    pulled = pullback(cotangent.astype(jnp.float32))[0].astype(jnp.bfloat16)
    local_bias = jnp.sum(pulled.astype(jnp.float32), axis=0)

    def weight_partial(pulled_rows):
        local_weight = jnp.einsum(
            "rnf,rng->fg",
            partial_ax.reshape(pulled_rows.shape),
            pulled_rows.astype(jnp.float32),
            precision=lax.Precision.HIGHEST,
            preferred_element_type=jnp.float32,
        )
        filler = jnp.zeros((7, local_bias.shape[0]), jnp.float32)
        return jnp.concatenate([local_weight, local_bias[None, :], filler], axis=0)

    gather_steps = blk_all_gather_steps()
    sum_steps = all_sum_steps()
    steps = gather_steps[1:-1] + [lambda cur: sum_steps[0](weight_partial(gather_steps[-1](cur)))]
    chain = Chain(gather_steps[0](pulled), steps + sum_steps[1:])
    pulled_group = gather_team(pulled, chain)
    partial_back = collect(pulled_group, slots, adj_vals)
    spread = blk_reduce_scatter(partial_back).astype(jnp.bfloat16)
    both = chain.finish()
    grad_input = jnp.dot(spread, weight.T, preferred_element_type=jnp.float32).astype(jnp.bfloat16)
    return (hidden, grad_input, both[:width], both[width])


def solution(mesh):
    fine = fine_mesh(mesh)
    rows = P(ALL_AXES, None)
    return jax.shard_map(
        local,
        mesh=fine,
        in_specs=(
            rows,
            P(),
            P(),
            rows,
            P(TEAM_AXES, None, BLK_AXES, None),
            P(TEAM_AXES, None, BLK_AXES, None, None, None),
        ),
        out_specs=(rows, rows, P(), P()),
        check_vma=False,
    )
```

```python
import functools

import jax
import jax.numpy as jnp
from jax import lax
from jax.experimental import pallas as pl
from jax.experimental.pallas import tpu as pltpu
from jax.sharding import Mesh
from jax.sharding import PartitionSpec as P

BLK_AXES = ("y_lo", "core")
TEAM_AXES = ("y_hi", "x", "z")
ALL_AXES = BLK_AXES + TEAM_AXES
SIZES = {}


def fine_mesh(mesh):
    blk = mesh.shape["blk"]
    team = mesh.shape["team"]
    sizes = (blk // 2, 2, 2, 4, team // 8)
    SIZES.update(zip(ALL_AXES, sizes))
    return Mesh(mesh.devices.reshape(sizes), ALL_AXES)


def ring_offsets(n):
    offsets = [0]
    for step in range(1, n // 2 + 1):
        offsets.append(-step)
        if step < n - step:
            offsets.append(step)
    return offsets


class Chain:
    def __init__(self, value, steps):
        self.value = value
        self.steps = list(steps)

    def tick(self, values, count=1):
        for _ in range(count):
            if self.steps:
                self.value = self.steps.pop(0)(self.value)
        values, self.value = lax.optimization_barrier((values, self.value))
        return values

    def finish(self):
        while self.steps:
            self.value = self.steps.pop(0)(self.value)
        return self.value


def ring_gather(blocks, axis, chain=None, per_round=1, join=True):
    n = SIZES[axis]
    ahead = blocks
    behind = blocks
    parts = [blocks]
    for step in range(1, n // 2 + 1):
        ahead = lax.ppermute(ahead, axis, [(i, (i + 1) % n) for i in range(n)])
        if step < n - step:
            behind = lax.ppermute(behind, axis, [(i, (i - 1) % n) for i in range(n)])
        if chain is not None:
            ahead, behind = chain.tick((ahead, behind), per_round)
        parts.append(ahead)
        if step < n - step:
            parts.append(behind)
    return jnp.concatenate(parts, axis=0) if join else parts


def gather_team(rows, chain=None):
    other = lax.ppermute(rows, "y_hi", perm=[(0, 1), (1, 0)])
    if chain is not None:
        other = chain.tick(other)
    pair = jnp.stack([rows, other], axis=0)
    return ring_gather(ring_gather(pair, "x", chain, 2), "z", chain, 2, join=False)


def ring_slot(delta, axis):
    n = SIZES[axis]
    order = [o % n for o in ring_offsets(n)]
    table = [order.index(d) for d in range(n)]
    return jnp.asarray(table, jnp.int32)[(delta + n) % n]


def member_slots(members):
    nx, nz = SIZES["x"], SIZES["z"]
    m_hi = members // (nx * nz)
    m_x = (members // nz) % nx
    m_z = members % nz
    y_slot = (m_hi != lax.axis_index("y_hi")).astype(jnp.int32)
    x_slot = ring_slot(m_x - lax.axis_index("x"), "x")
    z_slot = ring_slot(m_z - lax.axis_index("z"), "z")
    return (z_slot * nx + x_slot) * 2 + y_slot


def swap(value, axis, bit):
    n = SIZES[axis]
    return lax.ppermute(value, axis, [(i, i ^ bit) for i in range(n)])


BUTTERFLY = (("y_lo", 1), ("x", 1), ("z", 1), ("y_lo", 2), ("x", 2), ("z", 2), ("z", 4), ("y_hi", 1))


def all_sum_steps():
    def split(value):
        half = value.shape[0] // 2
        upper = lax.axis_index("core") == 1
        keep = jnp.where(upper, value[half:], value[:half])
        send = jnp.where(upper, value[:half], value[half:])
        return keep + swap(send, "core", 1)

    def join(part):
        upper = lax.axis_index("core") == 1
        other = swap(part, "core", 1)
        return jnp.where(upper, jnp.concatenate([other, part]), jnp.concatenate([part, other]))

    steps = [split]
    for axis, bit in BUTTERFLY:
        if bit < SIZES[axis]:
            steps.append(lambda part, axis=axis, bit=bit: part + swap(part, axis, bit))
    steps.append(join)
    return steps


def blk_reduce_scatter(partial):
    width = partial.shape[-1]
    block = partial.shape[0] // (SIZES["y_lo"] * SIZES["core"])
    cur = partial.reshape(-1, 2, block, width)
    upper = lax.axis_index("core") == 1
    keep = jnp.where(upper, cur[:, 1], cur[:, 0])
    send = jnp.where(upper, cur[:, 0], cur[:, 1])
    cur = keep + swap(send, "core", 1)
    bit = 1
    while bit < SIZES["y_lo"]:
        cur = cur.reshape(-1, 2, block, width)
        upper = (lax.axis_index("y_lo") & bit) != 0
        keep = jnp.where(upper, cur[:, 1], cur[:, 0])
        send = jnp.where(upper, cur[:, 0], cur[:, 1])
        cur = keep + swap(send, "y_lo", bit)
        bit *= 2
    return cur.reshape(block, width)


def blk_all_gather_steps():
    steps = [lambda rows: rows[None]]
    bit = 1
    while bit < SIZES["y_lo"]:
        def double(cur, bit=bit):
            upper = (lax.axis_index("y_lo") & bit) != 0
            got = swap(cur, "y_lo", bit)
            return jnp.where(upper, jnp.concatenate([got, cur]), jnp.concatenate([cur, got]))
        steps.append(double)
        bit *= 2

    def cores(cur):
        upper = lax.axis_index("core") == 1
        got = swap(cur, "core", 1)
        both = jnp.where(upper, jnp.stack([got, cur], axis=1), jnp.stack([cur, got], axis=1))
        return both.reshape((-1,) + cur.shape[1:])

    steps.append(cores)
    return steps


def collect_kernel(count, slots_ref, vals_ref, *refs):
    parts = refs[:count]
    out_ref, held, sems = refs[count:]
    row = pl.program_id(0)
    nnz = vals_ref.shape[0]
    size = held.shape[0] // count

    @pl.when(row == 0)
    def _():
        copies = [
            pltpu.make_async_copy(parts[i], held.at[pl.ds(i * size, size)], sems.at[i])
            for i in range(count)
        ]
        for copy in copies:
            copy.start()
        for copy in copies:
            copy.wait()

    total = jnp.zeros(out_ref.shape, jnp.float32)
    for k in range(nnz):
        slot = slots_ref[row * nnz + k]
        total = total + jnp.dot(vals_ref[k], held[slot], preferred_element_type=jnp.float32)
    out_ref[...] = total


def collect(parts, slots, adj_vals):
    block = adj_vals.shape[-1]
    width = parts[0].shape[-1]
    rows, nnz = slots.shape
    count = len(parts)
    panels = count * parts[0].shape[0]
    grid_spec = pltpu.PrefetchScalarGridSpec(
        num_scalar_prefetch=1,
        grid=(rows,),
        in_specs=[pl.BlockSpec((None, None, None, nnz, block, block), lambda r, s: (0, r, 0, 0, 0, 0))]
        + [pl.BlockSpec(memory_space=pl.ANY)] * count,
        out_specs=pl.BlockSpec((block, width), lambda r, s: (r, 0)),
        scratch_shapes=[
            pltpu.VMEM((panels, block, width), parts[0].dtype),
            pltpu.SemaphoreType.DMA((count,)),
        ],
    )
    return pl.pallas_call(
        functools.partial(collect_kernel, count),
        grid_spec=grid_spec,
        out_shape=jax.ShapeDtypeStruct((rows * block, width), jnp.float32),
        compiler_params=pltpu.CompilerParams(dimension_semantics=("arbitrary",)),
        cost_estimate=pl.CostEstimate(
            flops=2 * rows * nnz * block * block * width,
            transcendentals=0,
            bytes_accessed=panels * block * width * 2 + rows * nnz * block * block * 2 + rows * block * width * 4,
        ),
    )(slots.reshape(-1), adj_vals, *parts)


def activation(value):
    return jax.nn.gelu(value, approximate=True)


def local(features, weight, bias, cotangent, adj_cols, adj_vals):
    slots = member_slots(adj_cols[0, :, 0, :])
    width = features.shape[1]
    gathered = gather_team(features)
    partial_ax = collect(gathered, slots, adj_vals)
    partial_rows = jnp.dot(
        partial_ax,
        weight.astype(jnp.float32),
        precision=lax.Precision.HIGHEST,
        preferred_element_type=jnp.float32,
    )
    summed = blk_reduce_scatter(partial_rows)
    pre = summed + bias[None, :]
    activated, pullback = jax.vjp(activation, pre)
    hidden = activated.astype(jnp.bfloat16)
    pulled = pullback(cotangent.astype(jnp.float32))[0].astype(jnp.bfloat16)
    local_bias = jnp.sum(pulled.astype(jnp.float32), axis=0)

    def weight_partial(pulled_rows):
        local_weight = jnp.einsum(
            "rnf,rng->fg",
            partial_ax.reshape(pulled_rows.shape),
            pulled_rows.astype(jnp.float32),
            precision=lax.Precision.HIGHEST,
            preferred_element_type=jnp.float32,
        )
        filler = jnp.zeros((7, local_bias.shape[0]), jnp.float32)
        return jnp.concatenate([local_weight, local_bias[None, :], filler], axis=0)

    gather_steps = blk_all_gather_steps()
    sum_steps = all_sum_steps()
    steps = gather_steps[1:-1] + [lambda cur: sum_steps[0](weight_partial(gather_steps[-1](cur)))]
    chain = Chain(gather_steps[0](pulled), steps + sum_steps[1:])
    pulled_group = gather_team(pulled, chain)
    partial_back = collect(pulled_group, slots, adj_vals)
    spread = blk_reduce_scatter(partial_back).astype(jnp.bfloat16)
    both = chain.finish()
    grad_input = jnp.dot(spread, weight.T, preferred_element_type=jnp.float32).astype(jnp.bfloat16)
    return (hidden, grad_input, both[:width], both[width])


def solution(mesh):
    fine = fine_mesh(mesh)
    rows = P(ALL_AXES, None)
    return jax.shard_map(
        local,
        mesh=fine,
        in_specs=(
            rows,
            P(),
            P(),
            rows,
            P(TEAM_AXES, None, BLK_AXES, None),
            P(TEAM_AXES, None, BLK_AXES, None, None, None),
        ),
        out_specs=(rows, rows, P(), P()),
        check_vma=False,
    )
```
